256 devices in a mesh: member: 8 (over x, y_hi), tile: 32 (over z, y_lo, core).
Axes of the slice: x: 4, y: 4 (y_hi: 2, y_lo: 2; y = y_hi * 2 + y_lo), z: 8, core: 2. Of those that a mesh axis runs over, the one named last changes fastest.
Arguments:
- precip: float32 [4096, 256], P(('member', 'tile')), parts along dimension 0, may hold values from 0.2 to 2
- pet: float32 [4096, 256], P(('member', 'tile')), parts along dimension 0, may hold values from 0.05 to 0.5
- soil_init: float32 [4096, 256], P(('member', 'tile')), parts along dimension 0, may hold values from 0.05 to 0.4
- ksat: float32 [4096, 256], P(('member', 'tile')), parts along dimension 0, may hold values from 0.5 to 3
- land_mask: int32 [4096, 256], P(('member', 'tile')), parts along dimension 0, may hold values 0 or 1
- head_init: float32 [8192, 2048], P(('member', 'tile')), parts along dimension 0, may hold values from 0.2 to 2
- subsurface_init: float32 [8192, 2048], P(('member', 'tile')), parts along dimension 0, may hold values from 0.2 to 2
- conduct: float32 [8192, 2048], P(('member', 'tile')), parts along dimension 0, may hold values from 0.22 to 0.47
- drain_rate: float32 [8192, 2048], P(('member', 'tile')), parts along dimension 0, may hold values from 0.05 to 0.4
- flow_code: int32 [8192, 2048], P(('member', 'tile')), parts along dimension 0, may hold values from 0 to 3
- channel_share: float32 [8192, 2048], P(('member', 'tile')), parts along dimension 0, may hold values from 0.02 to 0.2
- cell_slot: int32 [8192, 2048], P(('member', 'tile')), parts along dimension 0, may hold values from 0 to 2047
- slot_reach: int32 [524288], P(('member', 'tile')), parts along dimension 0, may hold values from 0 to 2047
Outputs:
- soil: float32 [4096, 256], P(('member', 'tile')), parts along dimension 0
- head: float32 [8192, 2048], P(('member', 'tile')), parts along dimension 0
- subsurface: float32 [8192, 2048], P(('member', 'tile')), parts along dimension 0
- reach_inflow: float32 [524288], P(('member', 'tile')), parts along dimension 0
The draws below stay inside these ranges and needn't reach their ends.
There are 8 independent parts, one for each index of `member`. The reference program is written for one: setup_inputs(seed, part) draws one part's arguments, and reference() takes and returns one part's arrays. A program takes and returns all parts, laid end to end along the dimension named above; each array names one. Nothing has to cross between parts.
Inputs may be any that keep to these rules, and one draw needn't show every extreme that they name: `slot_reach`: slot k of a tile holds a reach owned by tile index k // 64.
All inputs are finite; a program needn't handle non-finite values. No bound on the sum of `land_mask` on one device may be relied on, other than what follows from the above.
Results may differ from the reference program's by a relative error of at most 0.00002.
Values sent between devices are 32-bit elements; how exact they have to be, the bound alone decides.
No kernel may reach another device: no remote copies, remote signals or barrier semaphores. Data moves between devices by JAX's collectives and lax.ppermute only.
A program may use at most 64 MiB of HBM per device.

```python
import math
import jax
import jax.numpy as jnp

FR_DEV = 32
FC = 2048
ITERS = 6
PER_OWNER = 64
REACH_DEV = 2048
FR = 1024
CC = 512
CR = 256
SLOTS = 2048
N_TILE = 32


def set_ends(entries, key, least, largest):
    dims = entries.shape
    spot = [jax.random.randint(jax.random.fold_in(key, axis), (), 0, dims[axis]) for axis in range(len(dims))]
    entries = entries.at[tuple(spot)].set(least)
    longest = dims.index(max(dims))
    spot[longest] = (spot[longest] + 1) % dims[longest]
    return entries.at[tuple(spot)].set(largest)


def shard_levels(stream_key, extent, shards, least, largest):
    gain, own = 1.0, jax.random.fold_in(stream_key, 6)
    for position, blocks in shards:
        steps = jnp.exp(jax.random.uniform(jax.random.fold_in(own, position), (blocks,), jnp.float32, least / len(shards), largest / len(shards)))
        gain = gain * jnp.repeat(steps, extent[position] // blocks).reshape([-1 if axis == position else 1 for axis in range(len(extent))])
    return gain


def setup_inputs(seed: int = 0, part: int = 0) -> dict:
    keys = jax.random.split(jax.random.key(seed), 14)
    part_keys = jax.random.split(jax.random.fold_in(keys[13], part), 14)
    return {
        "precip": jnp.clip(jnp.exp(math.log(2.0) - 2.3025851 * jax.random.uniform(part_keys[0], (CC, CR), jnp.float32) ** shard_levels(part_keys[0], (CC, CR), ((0, 32),), -0.2, 0.2)), 0.2, 2.0),
        "pet": jnp.clip(jnp.exp(math.log(0.5) - 2.3025851 * jax.random.uniform(part_keys[1], (CC, CR), jnp.float32) ** shard_levels(part_keys[1], (CC, CR), ((0, 32),), -0.2, 0.2)), 0.05, 0.5),
        "soil_init": jnp.clip(0.05 + 0.35 * jax.random.uniform(part_keys[2], (CC, CR), jnp.float32) ** shard_levels(part_keys[2], (CC, CR), ((0, 32),), -0.2, 0.2), 0.05, 0.4),
        "ksat": jnp.clip(jnp.exp(math.log(3.0) - 1.7917595 * jax.random.uniform(part_keys[3], (CC, CR), jnp.float32) ** shard_levels(part_keys[3], (CC, CR), ((0, 32),), -0.2, 0.2)), 0.5, 3.0),
        "land_mask": set_ends((jax.random.randint(part_keys[4], (CC, CR), 0, 4) < 3).astype(jnp.int32), jax.random.fold_in(part_keys[4], 1), 0, 1),
        "head_init": jnp.clip(jnp.exp(math.log(2.0) - 2.3025851 * jax.random.uniform(part_keys[5], (FR, FC), jnp.float32) ** shard_levels(part_keys[5], (FR, FC), ((0, 32),), -0.2, 0.2)), 0.2, 2.0),
        "subsurface_init": jnp.clip(jnp.exp(math.log(2.0) - 2.3025851 * jax.random.uniform(part_keys[6], (FR, FC), jnp.float32) ** shard_levels(part_keys[6], (FR, FC), ((0, 32),), -0.2, 0.2)), 0.2, 2.0),
        "conduct": jnp.clip(jnp.exp(math.log(0.47) - 0.75910515 * jax.random.uniform(part_keys[7], (FR, FC), jnp.float32) ** shard_levels(part_keys[7], (FR, FC), ((0, 32),), -0.2, 0.2)), 0.22, 0.47),
        "drain_rate": jnp.clip(jnp.exp(math.log(0.4) - 2.0794415 * jax.random.uniform(part_keys[8], (FR, FC), jnp.float32) ** shard_levels(part_keys[8], (FR, FC), ((0, 32),), -0.2, 0.2)), 0.05, 0.4),
        "flow_code": set_ends(jax.random.randint(part_keys[9], (FR, FC), 0, 4), jax.random.fold_in(part_keys[9], 1), 0, 3).astype(jnp.int32),
        "channel_share": jnp.clip(0.02 + 0.18 * jax.random.uniform(part_keys[10], (FR, FC), jnp.float32) ** shard_levels(part_keys[10], (FR, FC), ((0, 32),), -0.2, 0.2), 0.02, 0.2),
        "cell_slot": set_ends(jax.random.randint(part_keys[11], (FR, FC), 0, SLOTS), jax.random.fold_in(part_keys[11], 1), 0, SLOTS - 1).astype(jnp.int32),
        "slot_reach": set_ends(jax.random.randint(part_keys[12], (N_TILE * SLOTS,), 0, REACH_DEV), jax.random.fold_in(part_keys[12], 1), 0, REACH_DEV - 1).astype(jnp.int32),
    }


def land_step(precip, pet, soil_init, ksat, land_mask):
    mask = land_mask.astype(jnp.float32)
    wet = 2.0 * soil_init
    cap = ksat * (1.0 - wet)
    runoff = mask * precip * precip / (precip + cap)
    drainage = 0.25 * mask * ksat * wet ** 4
    evap = mask * pet * wet
    soil = soil_init + 0.1 * (mask * precip - runoff - drainage - evap)
    return soil, runoff, drainage


def advance(state, statics):
    h = state[0]
    s = state[1]
    g, down, up, right, left = statics[0], statics[1], statics[2], statics[3], statics[4]
    hc = h[1:-1]
    gc = g[1:-1]
    sc = s[1:-1]
    hs = jnp.pad(hc, ((0, 0), (1, 1)))
    gs = jnp.pad(gc, ((0, 0), (1, 1)))
    flux = g[:-2] * (h[:-2] - hc) + g[2:] * (h[2:] - hc)
    flux = flux + gs[:, :-2] * (hs[:, :-2] - hc) + gs[:, 2:] * (hs[:, 2:] - hc)
    h_new = hc + gc * flux
    moving_right = jnp.pad((right * s)[1:-1], ((0, 0), (1, 1)))
    moving_left = jnp.pad((left * s)[1:-1], ((0, 0), (1, 1)))
    incoming = (down * s)[:-2] + (up * s)[2:] + moving_right[:, :-2] + moving_left[:, 2:]
    outgoing = (down + up + right + left)[1:-1]
    s_new = sc - outgoing * sc + incoming
    return jnp.stack([h_new, s_new])


def make_statics(conduct, drain_rate, flow_code):
    parts = [conduct]
    for code in range(4):
        parts.append(drain_rate * (flow_code == code).astype(jnp.float32))
    return jnp.stack(parts)


def reference(precip, pet, soil_init, ksat, land_mask, head_init, subsurface_init, conduct, drain_rate, flow_code, channel_share, cell_slot, slot_reach):
    soil, runoff, drainage = land_step(precip, pet, soil_init, ksat, land_mask)
    fine = jnp.stack([runoff.T, drainage.T])
    fine = jnp.repeat(jnp.repeat(fine, 4, axis=1), 4, axis=2)
    state = jnp.stack([head_init + fine[0], subsurface_init + fine[1]])
    statics = jnp.pad(make_statics(conduct, drain_rate, flow_code), ((0, 0), (1, 1), (0, 0)))
    for step in range(ITERS):
        state = advance(jnp.pad(state, ((0, 0), (1, 1), (0, 0))), statics)
    h = state[0]
    inflow = channel_share * h
    head = h - inflow
    rows = jnp.arange(FR, dtype=jnp.int32) // FR_DEV
    slots = PER_OWNER * N_TILE
    place = slot_reach[(rows[:, None] * slots + cell_slot).astype(jnp.int32)]
    reach_id = (cell_slot // PER_OWNER) * REACH_DEV + place
    reach_inflow = jax.ops.segment_sum(inflow.ravel(), reach_id.ravel().astype(jnp.int32), num_segments=REACH_DEV * N_TILE)
    return soil, head, state[1], reach_inflow
```

```python
import jax
import jax.numpy as jnp
from jax import lax
from jax.experimental import pallas as pl
from jax.experimental.pallas import tpu as pltpu
from jax.sharding import PartitionSpec as P

ITERS = 6
HALO = 8
LANES = 128
F32 = jnp.float32
BF16 = jnp.bfloat16


def iota(shape, dim):
    return lax.broadcasted_iota(jnp.int32, shape, dim)


def split3(x):
    a = x.astype(BF16).astype(F32)
    r = x - a
    b = r.astype(BF16).astype(F32)
    return a, b, r - b


def land_kernel(precip, pet, soil_init, ksat, land_mask, soil_out, msg, turned):
    mask = land_mask[...].astype(F32)
    p = precip[...]
    s0 = soil_init[...]
    k = ksat[...]
    wet = 2.0 * s0
    cap = k * (1.0 - wet)
    runoff = mask * p * p / (p + cap)
    wet2 = wet * wet
    drainage = 0.25 * mask * k * (wet2 * wet2)
    evap = mask * pet[...] * wet
    soil_out[...] = s0 + 0.1 * (mask * p - runoff - drainage - evap)
    rows = p.shape[1]
    fields = jnp.concatenate([runoff, drainage], axis=0)
    turned[0:8, :] = jnp.zeros((8, LANES), F32)
    turned[rows + 8 : rows + 16, :] = jnp.zeros((8, LANES), F32)
    turned[8 : rows + 8, :] = jnp.concatenate([fields] * 4, axis=0).T
    group = iota((32, LANES), 1) // 32
    for j in range(3):
        chunk = None
        for q in range(4):
            part = turned[pl.ds(6 + 4 * j + q, 32, stride=8), :]
            chunk = part if q == 0 else jnp.where(group == q, part, chunk)
        msg[:, LANES * j : LANES * (j + 1)] = chunk


def route_kernel(
    land, head_init, sub_init, conduct, drain, code, share, slot, places, above, below,
    head_out, sub_out, msg,
    turned, h_a, h_b, s_a, s_b, g_w, a_w, dn_w, up_w, rt_w, lf_w, kp_w, parts,
):
    width = head_init.shape[1]
    tiles = width // LANES
    rows = 32 + 2 * HALO
    lane = iota((rows, LANES), 1)
    first = lane == 0
    last = lane == LANES - 1
    zero = jnp.zeros((rows, LANES), F32)

    a, b, c = split3(land[...])
    stacked = jnp.concatenate([a, b, c, jnp.zeros_like(a)], axis=0)
    turned[...] = stacked.T
    lhs = jnp.concatenate([turned[pl.ds(q, 24, stride=16), :] for q in range(16)], axis=0)
    lhs = lhs.astype(BF16)
    low_half = iota((8, 256), 0) < 4
    src = iota((LANES, 256), 0)
    dst = iota((LANES, 256), 1)
    col = (iota((24, 256), 1) & 63) >> 2
    for n in range(width // 256):
        hot = ((src & 31) == ((dst + 256 * n) >> 6)) & (src < 96)
        spread = jnp.dot(lhs, jnp.where(hot, 1.0, 0.0).astype(BF16), preferred_element_type=F32)
        fine = spread[0:24]
        for q in range(1, 16):
            fine = jnp.where(col == q, spread[24 * q : 24 * q + 24], fine)
        at = slice(256 * n, 256 * n + 256)
        for i in range(6):
            if i == 0:
                h0, s0 = above[0:8, at], above[8:16, at]
            elif i == 5:
                h0, s0 = below[0:8, at], below[8:16, at]
            else:
                h0, s0 = head_init[8 * i - 8 : 8 * i, at], sub_init[8 * i - 8 : 8 * i, at]
            here = slice(8 * i, 8 * i + 8)
            h_a[here, at] = h0 + jnp.where(low_half, fine[4 * i : 4 * i + 1], fine[4 * i + 2 : 4 * i + 3])
            s_a[here, at] = s0 + jnp.where(low_half, fine[4 * i + 1 : 4 * i + 2], fine[4 * i + 3 : 4 * i + 4])

    def window(own, field, at):
        lo = 8 * field
        return jnp.concatenate([above[lo : lo + 8, at], own[:, at], below[lo : lo + 8, at]], axis=0)

    def cut(j):
        return slice(LANES * j, LANES * (j + 1))

    for j in range(tiles):
        at = cut(j)
        d = window(drain, 3, at)
        k = jnp.concatenate(
            [above[32:40, at], code[:, at].astype(F32), below[32:40, at]], axis=0
        )
        moves = []
        for value, ref in ((0.0, dn_w), (1.0, up_w), (2.0, rt_w), (3.0, lf_w)):
            part = jnp.where(k == value, d, 0.0)
            ref[:, at] = part
            moves.append(part)
        kp_w[:, at] = 1.0 - (moves[0] + moves[1] + moves[2] + moves[3])
        g_w[:, at] = window(conduct, 2, at)
    for j in range(tiles):
        at = cut(j)
        g = g_w[:, at]
        left = pltpu.roll(g_w[:, cut(j - 1)], 1, 1) if j > 0 else zero
        right = pltpu.roll(g_w[:, cut(j + 1)], LANES - 1, 1) if j < tiles - 1 else zero
        total = pltpu.roll(g, 1, 0) + pltpu.roll(g, rows - 1, 0)
        total = total + jnp.where(first, left, pltpu.roll(g, 1, 1))
        total = total + jnp.where(last, right, pltpu.roll(g, LANES - 1, 1))
        a_w[:, at] = 1.0 - g * total

    def products(j, h_in, s_in):
        at = cut(j)
        p = g_w[:, at] * h_in[:, at]
        s = s_in[:, at]
        return (
            p,
            pltpu.roll(p, 1, 1),
            pltpu.roll(p, LANES - 1, 1),
            pltpu.roll(rt_w[:, at] * s, 1, 1),
            pltpu.roll(lf_w[:, at] * s, LANES - 1, 1),
        )

    def substep(h_in, s_in, h_to, s_to):
        before = (zero,) * 5
        now = products(0, h_in, s_in)
        for j in range(tiles):
            at = cut(j)
            after = products(j + 1, h_in, s_in) if j < tiles - 1 else (zero,) * 5
            p = now[0]
            s = s_in[:, at]
            flux = pltpu.roll(p, 1, 0) + pltpu.roll(p, rows - 1, 0)
            flux = flux + jnp.where(first, before[1], now[1])
            flux = flux + jnp.where(last, after[2], now[2])
            h_to[:, at] = a_w[:, at] * h_in[:, at] + g_w[:, at] * flux
            new = kp_w[:, at] * s
            new = new + pltpu.roll(dn_w[:, at] * s, 1, 0)
            new = new + pltpu.roll(up_w[:, at] * s, rows - 1, 0)
            new = new + jnp.where(first, before[3], now[3])
            new = new + jnp.where(last, after[4], now[4])
            s_to[:, at] = new
            before, now = now, after

    def pair(i, carry):
        substep(h_a, s_a, h_b, s_b)
        substep(h_b, s_b, h_a, s_a)
        return carry

    lax.fori_loop(0, ITERS // 2, pair, 0)

    own = slice(HALO, HALO + 32)
    sub_out[...] = s_a[own, :]
    for j in range(tiles):
        at = cut(j)
        h = h_a[own, at]
        inflow = share[:, at] * h
        head_out[:, at] = h - inflow
        v1, v2, v3 = split3(inflow)
        parts[0, :, at] = v1
        parts[1, :, at] = v2
        parts[2, :, at] = v3
        k = slot[:, at]
        parts[3, :, at] = (k >> 6).astype(F32)
        parts[4, :, at] = (k & 63).astype(F32)

    owner = iota((32, width), 0).astype(F32).astype(BF16)
    place = iota((64, width), 0).astype(F32).astype(BF16)
    one = jnp.ones((64, width), BF16)
    none64 = jnp.zeros((64, width), BF16)
    none32 = jnp.zeros((32, width), BF16)

    def row(r, total):
        def wide(i, n):
            return jnp.broadcast_to(parts[i, pl.ds(r, 1), :], (n, width)).astype(BF16)

        hi = wide(3, 32) == owner
        lhs = jnp.concatenate([jnp.where(hi, wide(i, 32), none32) for i in range(3)], axis=0)
        rhs = jnp.where(wide(4, 64) == place, one, none64)
        return total + lax.dot_general(lhs, rhs, (((1,), (1,)), ((), ())), preferred_element_type=F32)

    total = lax.fori_loop(0, 32, row, jnp.zeros((96, 64), F32))
    total = total[0:32] + total[32:64] + total[64:96]
    p = places[...].astype(F32)
    turned[pl.ds(0, 16, stride=2), :] = pltpu.roll(p, 64, 1)
    turned[pl.ds(1, 16, stride=2), :] = p
    wide = jnp.concatenate([total, jnp.zeros_like(total)], axis=1)
    msg[...] = jnp.where(iota((32, LANES), 1) < 64, wide, turned[0:32, :])


def reach_kernel(got, out, stage):
    data = got[...]
    valid = iota(data.shape, 1) < 64
    place = pltpu.roll(data, 64, 1).astype(jnp.int32)
    a, b, c = split3(jnp.where(valid, data, 0.0))
    stage[0] = a
    stage[1] = b
    stage[2] = c
    stage[3] = (place >> 7).astype(F32)
    stage[4] = (place & 127).astype(F32)
    hi_line = iota((16, LANES), 0).astype(F32)
    lo_line = iota((128, LANES), 0).astype(F32)
    total = jnp.zeros((48, LANES), F32)
    for u in range(data.shape[0]):
        hi = stage[3, u : u + 1, :] == hi_line
        lhs = jnp.concatenate(
            [jnp.where(hi, stage[i, u : u + 1, :], 0.0) for i in range(3)], axis=0
        ).astype(BF16)
        rhs = jnp.where(stage[4, u : u + 1, :] == lo_line, 1.0, 0.0).astype(BF16)
        total = total + lax.dot_general(
            lhs, rhs, (((1,), (1,)), ((), ())), preferred_element_type=F32
        )
    out[...] = total[0:16] + total[16:32] + total[32:48]


def local(
    precip,
    pet,
    soil_init,
    ksat,
    land_mask,
    head_init,
    subsurface_init,
    conduct,
    drain_rate,
    flow_code,
    channel_share,
    cell_slot,
    slot_reach,
):
    vmem = pl.BlockSpec(memory_space=pltpu.VMEM)
    peers = lax.axis_size("tile")
    width = head_init.shape[1]
    grid = (head_init, subsurface_init, conduct, drain_rate, flow_code)
    up = [(i, i + 1) for i in range(peers - 1)]
    down = [(j, i) for i, j in up]
    bottom = jnp.concatenate([x[-HALO:].astype(F32) for x in grid], axis=0)
    top = jnp.concatenate([x[:HALO].astype(F32) for x in grid], axis=0)
    above = lax.ppermute(bottom, "tile", up)
    below = lax.ppermute(top, "tile", down)

    soil, land = pl.pallas_call(
        land_kernel,
        out_shape=(
            jax.ShapeDtypeStruct(precip.shape, F32),
            jax.ShapeDtypeStruct((peers, 384), F32),
        ),
        in_specs=[vmem] * 5,
        out_specs=(vmem, vmem),
        scratch_shapes=[pltpu.VMEM((precip.shape[1] + 16, LANES), F32)],
        name="land_step",
    )(precip, pet, soil_init, ksat, land_mask)
    land = lax.all_to_all(land, "tile", split_axis=0, concat_axis=0, tiled=True)

    window = pltpu.VMEM((32 + 2 * HALO, width), F32)
    head, sub, sums = pl.pallas_call(
        route_kernel,
        out_shape=(
            jax.ShapeDtypeStruct(head_init.shape, F32),
            jax.ShapeDtypeStruct(head_init.shape, F32),
            jax.ShapeDtypeStruct((peers, LANES), F32),
        ),
        in_specs=[vmem] * 11,
        out_specs=(vmem, vmem, vmem),
        scratch_shapes=[pltpu.VMEM((384, LANES), F32)]
        + [window] * 11
        + [pltpu.VMEM((5, 32, width), F32)],
        compiler_params=pltpu.CompilerParams(vmem_limit_bytes=48 * 1024 * 1024),
        name="route",
    )(
        land, head_init, subsurface_init, conduct, drain_rate, flow_code, channel_share,
        cell_slot, slot_reach.reshape(-1, LANES), above, below,
    )
    sums = lax.all_to_all(sums, "tile", split_axis=0, concat_axis=0, tiled=True)
    reach = pl.pallas_call(
        reach_kernel,
        out_shape=jax.ShapeDtypeStruct((16, LANES), F32),
        in_specs=[vmem],
        out_specs=vmem,
        scratch_shapes=[pltpu.VMEM((5, peers, LANES), F32)],
        name="reach_sums",
    )(sums)
    return (soil, head, sub, reach.reshape(-1))


def solution(mesh):
    rows = P(("member", "tile"), None)
    flat = P(("member", "tile"))
    return jax.shard_map(
        local,
        mesh=mesh,
        in_specs=(rows,) * 12 + (flat,),
        out_specs=(rows, rows, rows, flat),
        check_vma=False,
    )
```

```python
import jax
import jax.numpy as jnp
from jax import lax
from jax.experimental import pallas as pl
from jax.experimental.pallas import tpu as pltpu
from jax.sharding import PartitionSpec as P

ITERS = 6
HALO = 8
OWN = 32
ROWS = OWN + 2 * HALO
LANES = 128
F32 = jnp.float32
BF16 = jnp.bfloat16
MIB = 1024 * 1024


def iota(shape, dim):
    return lax.broadcasted_iota(jnp.int32, shape, dim)


def split3(x):
    a = x.astype(BF16).astype(F32)
    r = x - a
    b = r.astype(BF16).astype(F32)
    return a, b, r - b


def cut(j):
    return slice(LANES * j, LANES * (j + 1))


def left_of(tile, before):
    return jnp.where(iota(tile.shape, 1) == 0, before, tile)


def right_of(tile, after):
    return jnp.where(iota(tile.shape, 1) == LANES - 1, after, tile)


def send_kernel(
    precip, pet, soil_init, ksat, land_mask, places, head, sub, conduct, drain, code,
    soil_out, msg, top, bottom, turned, fields_in, mask_in, place_in, code_edge, sem,
):
    local = []
    for i, ref in enumerate((precip, pet, soil_init, ksat)):
        local.append(pltpu.make_async_copy(ref, fields_in.at[i], sem.at[10 + i]))
    local.append(pltpu.make_async_copy(land_mask, mask_in, sem.at[14]))
    local.append(pltpu.make_async_copy(places, place_in, sem.at[15]))
    copies = []
    for i, ref in enumerate((head, sub, conduct, drain)):
        into = slice(8 * i, 8 * i + 8)
        copies.append(pltpu.make_async_copy(ref.at[24:32, :], bottom.at[into, :], sem.at[2 * i]))
        copies.append(pltpu.make_async_copy(ref.at[0:8, :], top.at[into, :], sem.at[2 * i + 1]))
    codes = (
        pltpu.make_async_copy(code.at[24:32, :], code_edge.at[0], sem.at[8]),
        pltpu.make_async_copy(code.at[0:8, :], code_edge.at[1], sem.at[9]),
    )
    for c in local:
        c.start()
    for c in codes:
        c.start()
    for c in copies:
        c.start()
    for c in local:
        c.wait()
    mask = mask_in[...].astype(F32)
    p = fields_in[0]
    s0 = fields_in[2]
    k = fields_in[3]
    wet = 2.0 * s0
    cap = k * (1.0 - wet)
    runoff = mask * p * p / (p + cap)
    wet2 = wet * wet
    drainage = 0.25 * mask * k * (wet2 * wet2)
    evap = mask * fields_in[1] * wet
    soil_out[...] = s0 + 0.1 * (mask * p - runoff - drainage - evap)
    rows = p.shape[1]
    fields = jnp.concatenate([runoff, drainage], axis=0)
    turned[0:8, :] = jnp.zeros((8, LANES), F32)
    turned[rows + 8 : rows + 16, :] = jnp.zeros((8, LANES), F32)
    turned[8 : rows + 8, :] = jnp.concatenate([fields] * 4, axis=0).T
    group = iota((32, LANES), 1) // 32
    for j in range(3):
        chunk = None
        for q in range(4):
            part = turned[pl.ds(6 + 4 * j + q, 32, stride=8), :]
            chunk = part if q == 0 else jnp.where(group == q, part, chunk)
        msg[pl.ds(j, 32, stride=4), :] = chunk
    place = place_in[...].astype(F32)
    msg[pl.ds(3, 16, stride=8), :] = place
    msg[pl.ds(7, 16, stride=8), :] = pltpu.roll(place, 64, 1)
    for c in codes:
        c.wait()
    bottom[32:40, :] = code_edge[0].astype(F32)
    top[32:40, :] = code_edge[1].astype(F32)
    for c in copies:
        c.wait()


def route_kernel(
    land, head_init, sub_init, conduct, drain, code, above, below, share, slot,
    head_out, sub_out, msg,
    turned, h_a, h_b, s_a, s_b, g_w, a_w, dn_w, up_w, rt_w, lf_w, kp_w,
    head, sub, shares, slots, parts, sem,
):
    tiles = g_w.shape[0]
    width = tiles * LANES
    zero = jnp.zeros((ROWS, LANES), F32)
    share_copy = pltpu.make_async_copy(share, shares, sem.at[0])
    slot_copy = pltpu.make_async_copy(slot, slots, sem.at[3])
    share_copy.start()
    slot_copy.start()

    def window(own, field, j):
        lo = 8 * field
        at = cut(j)
        return jnp.concatenate(
            [above[lo : lo + 8, at], own[:, at].astype(F32), below[lo : lo + 8, at]], axis=0
        )

    for j in range(tiles):
        g_w[j] = window(conduct, 2, j)
        d = window(drain, 3, j)
        k = window(code, 4, j)
        moves = [jnp.where(k == float(i), d, 0.0) for i in range(4)]
        dn_w[j], up_w[j], rt_w[j], lf_w[j] = moves
        kp_w[j] = 1.0 - (moves[0] + moves[1] + moves[2] + moves[3])
    for j in range(tiles):
        g = g_w[j]
        left = pltpu.roll(g_w[j - 1], 1, 1) if j > 0 else zero
        right = pltpu.roll(g_w[j + 1], LANES - 1, 1) if j < tiles - 1 else zero
        total = pltpu.roll(g, 1, 0) + pltpu.roll(g, ROWS - 1, 0)
        total = total + left_of(pltpu.roll(g, 1, 1), left)
        total = total + right_of(pltpu.roll(g, LANES - 1, 1), right)
        a_w[j] = 1.0 - g * total

    data = jnp.concatenate([land[pl.ds(j, 32, stride=4), :] for j in range(3)], axis=1)
    a, b, c = split3(data)
    turned[...] = jnp.concatenate([a, b, c, jnp.zeros_like(a)], axis=0).T
    lhs = jnp.concatenate([turned[pl.ds(q, 24, stride=16), :] for q in range(16)], axis=0)
    lhs = lhs.astype(BF16)
    low_half = iota((8, 256), 0) < 4
    src = iota((LANES, 256), 0)
    dst = iota((LANES, 256), 1)
    col = (iota((24, 256), 1) & 63) >> 2
    for n in range(width // 256):
        hot = ((src & 31) == ((dst + 256 * n) >> 6)) & (src < 96)
        spread = jnp.dot(lhs, jnp.where(hot, 1.0, 0.0).astype(BF16), preferred_element_type=F32)
        fine = spread[0:24]
        for q in range(1, 16):
            fine = jnp.where(col == q, spread[24 * q : 24 * q + 24], fine)
        for i in range(ROWS // 8):
            here = slice(8 * i, 8 * i + 8)
            at = slice(256 * n, 256 * n + 256)
            if i == 0:
                h0, s0 = above[0:8, at], above[8:16, at]
            elif i == ROWS // 8 - 1:
                h0, s0 = below[0:8, at], below[8:16, at]
            else:
                rows = slice(8 * i - 8, 8 * i)
                h0, s0 = head_init[rows, at], sub_init[rows, at]
            r = 4 * i
            h0 = h0 + jnp.where(low_half, fine[r : r + 1], fine[r + 2 : r + 3])
            s0 = s0 + jnp.where(low_half, fine[r + 1 : r + 2], fine[r + 3 : r + 4])
            for u in range(2):
                j = 2 * n + u
                h_a[j, here, :] = h0[:, cut(u)]
                s_a[j, here, :] = s0[:, cut(u)]

    def products(j, h_in, s_in):
        p = g_w[j] * h_in[j]
        s = s_in[j]
        return (
            p,
            pltpu.roll(p, 1, 1),
            pltpu.roll(p, LANES - 1, 1),
            pltpu.roll(rt_w[j] * s, 1, 1),
            pltpu.roll(lf_w[j] * s, LANES - 1, 1),
        )

    def substep(h_in, s_in, h_to, s_to):
        before = (zero,) * 5
        now = products(0, h_in, s_in)
        for j in range(tiles):
            after = products(j + 1, h_in, s_in) if j < tiles - 1 else (zero,) * 5
            p = now[0]
            s = s_in[j]
            flux = pltpu.roll(p, 1, 0) + pltpu.roll(p, ROWS - 1, 0)
            flux = flux + left_of(now[1], before[1])
            flux = flux + right_of(now[2], after[2])
            h_to[j] = a_w[j] * h_in[j] + g_w[j] * flux
            new = pltpu.roll(dn_w[j] * s, 1, 0) + pltpu.roll(up_w[j] * s, ROWS - 1, 0)
            new = new + kp_w[j] * s
            new = new + left_of(now[3], before[3])
            s_to[j] = new + right_of(now[4], after[4])
            before, now = now, after

    for i in range(ITERS // 2):
        substep(h_a, s_a, h_b, s_b)
        substep(h_b, s_b, h_a, s_a)

    share_copy.wait()
    slot_copy.wait()
    for j in range(tiles):
        at = cut(j)
        h = h_a[j, HALO : HALO + OWN, :]
        sub[:, at] = s_a[j, HALO : HALO + OWN, :]
        inflow = shares[:, at] * h
        head[:, at] = h - inflow
        parts[0, :, at], parts[1, :, at], parts[2, :, at] = split3(inflow)
        q = slots[:, at]
        parts[3, :, at] = (q >> 6).astype(F32)
        parts[4, :, at] = (q & 63).astype(F32)
    head_copy = pltpu.make_async_copy(head, head_out, sem.at[1])
    sub_copy = pltpu.make_async_copy(sub, sub_out, sem.at[2])
    head_copy.start()
    sub_copy.start()

    owner = iota((32, width), 0).astype(F32).astype(BF16)
    place = iota((64, width), 0).astype(F32).astype(BF16)
    one = jnp.ones((64, width), BF16)
    none64 = jnp.zeros((64, width), BF16)
    none32 = jnp.zeros((32, width), BF16)

    def wide(row, n):
        return jnp.broadcast_to(row, (n, width)).astype(BF16)

    total = jnp.zeros((96, 64), F32)
    for r in range(OWN):
        at = slice(r, r + 1)
        hi = wide(parts[3, at, :], 32) == owner
        lhs = jnp.concatenate(
            [jnp.where(hi, wide(parts[i, at, :], 32), none32) for i in range(3)], axis=0
        )
        rhs = jnp.where(wide(parts[4, at, :], 64) == place, one, none64)
        total = total + lax.dot_general(
            lhs, rhs, (((1,), (1,)), ((), ())), preferred_element_type=F32
        )
    total = total[0:32] + total[32:64] + total[64:96]
    msg[...] = jnp.concatenate([total, jnp.zeros_like(total)], axis=1)
    head_copy.wait()
    sub_copy.wait()


def reach_kernel(land, got, out):
    low = iota((16, LANES), 1) < 64

    def pack(x):
        return jnp.where(low, x[0:16], pltpu.roll(x[16:32], 64, 1))

    sums = pack(got[...])
    place = pack(land[pl.ds(3, 32, stride=4), :]).astype(jnp.int32)

    def line(x):
        return jnp.concatenate([x[u : u + 1] for u in range(16)], axis=1)

    width = 16 * LANES
    hi = line((place >> 7).astype(F32)) == iota((16, width), 0).astype(F32)
    lhs = jnp.concatenate([jnp.where(hi, line(x), 0.0) for x in split3(sums)], axis=0)
    lo = line((place & 127).astype(F32)) == iota((LANES, width), 0).astype(F32)
    total = lax.dot_general(
        lhs.astype(BF16), jnp.where(lo, 1.0, 0.0).astype(BF16),
        (((1,), (1,)), ((), ())), preferred_element_type=F32,
    )
    out[...] = total[0:16] + total[16:32] + total[32:48]


def local(
    precip,
    pet,
    soil_init,
    ksat,
    land_mask,
    head_init,
    subsurface_init,
    conduct,
    drain_rate,
    flow_code,
    channel_share,
    cell_slot,
    slot_reach,
):
    vmem = pl.BlockSpec(memory_space=pltpu.VMEM)
    far = pl.BlockSpec(memory_space=pltpu.HBM)
    peers = lax.axis_size("tile")
    width = head_init.shape[1]
    tiles = width // LANES

    def hbm(x):
        return pltpu.with_memory_space_constraint(x, pltpu.HBM)

    def array(*shape):
        return jax.ShapeDtypeStruct(shape, F32)

    soil, msg, top, bottom = pl.pallas_call(
        send_kernel,
        out_shape=(
            array(*precip.shape), array(4 * peers, LANES), array(40, width), array(40, width),
        ),
        in_specs=[far] * 11,
        out_specs=(vmem,) * 4,
        scratch_shapes=[
            pltpu.VMEM((precip.shape[1] + 16, LANES), F32),
            pltpu.VMEM((4,) + precip.shape, F32),
            pltpu.VMEM(precip.shape, jnp.int32),
            pltpu.VMEM((16, LANES), jnp.int32),
            pltpu.VMEM((2, 8, width), jnp.int32),
            pltpu.SemaphoreType.DMA((16,)),
        ],
        compiler_params=pltpu.CompilerParams(vmem_limit_bytes=6 * MIB),
        name="send",
    )(
        *map(
            hbm,
            (
                precip, pet, soil_init, ksat, land_mask, slot_reach.reshape(-1, LANES),
                head_init, subsurface_init, conduct, drain_rate, flow_code,
            ),
        )
    )
    up = [(i, i + 1) for i in range(peers - 1)]
    down = [(j, i) for i, j in up]
    above = lax.ppermute(bottom, "tile", up)
    below = lax.ppermute(top, "tile", down)
    land = lax.all_to_all(
        msg.reshape(peers, 4, LANES), "tile", split_axis=0, concat_axis=0, tiled=True
    ).reshape(4 * peers, LANES)

    window = pltpu.VMEM((tiles, ROWS, LANES), F32)
    plane = pltpu.VMEM((OWN, width), F32)
    head, sub, sums = pl.pallas_call(
        route_kernel,
        out_shape=(array(OWN, width), array(OWN, width), array(peers, LANES)),
        in_specs=[vmem] * 8 + [far] * 2,
        out_specs=(far, far, vmem),
        scratch_shapes=[pltpu.VMEM((384, LANES), F32)]
        + [window] * 11
        + [plane] * 3
        + [pltpu.VMEM((OWN, width), jnp.int32), pltpu.VMEM((5, OWN, width), F32)]
        + [pltpu.SemaphoreType.DMA((4,))],
        compiler_params=pltpu.CompilerParams(vmem_limit_bytes=16 * MIB),
        name="route",
    )(
        land, head_init, subsurface_init, conduct, drain_rate, flow_code, above, below,
        hbm(channel_share), hbm(cell_slot),
    )
    sums = lax.all_to_all(sums, "tile", split_axis=0, concat_axis=0, tiled=True)
    reach = pl.pallas_call(
        reach_kernel,
        out_shape=array(16, LANES),
        in_specs=[vmem] * 2,
        out_specs=vmem,
        compiler_params=pltpu.CompilerParams(vmem_limit_bytes=6 * MIB),
        name="reach_sums",
    )(land, sums)
    return (soil, head, sub, reach.reshape(-1))


def solution(mesh):
    rows = P(("member", "tile"), None)
    flat = P(("member", "tile"))
    return jax.shard_map(
        local,
        mesh=mesh,
        in_specs=(rows,) * 12 + (flat,),
        out_specs=(rows, rows, rows, flat),
        check_vma=False,
    )
```

```python
import jax
import jax.numpy as jnp
from jax import lax
from jax.experimental import pallas as pl
from jax.experimental.pallas import tpu as pltpu
from jax.sharding import PartitionSpec as P

ITERS = 6
HALO = 8
OWN = 32
ROWS = OWN + 2 * HALO
LANES = 128
F32 = jnp.float32
BF16 = jnp.bfloat16
MIB = 1024 * 1024


def iota(shape, dim):
    return lax.broadcasted_iota(jnp.int32, shape, dim)


def split3(x):
    a = x.astype(BF16).astype(F32)
    r = x - a
    b = r.astype(BF16).astype(F32)
    return a, b, r - b


def cut(j):
    return slice(LANES * j, LANES * (j + 1))


def left_of(tile, before):
    return jnp.where(iota(tile.shape, 1) == 0, before, tile)


def right_of(tile, after):
    return jnp.where(iota(tile.shape, 1) == LANES - 1, after, tile)


def land_kernel(
    precip, pet, soil_init, ksat, land_mask, places,
    soil_out, msg, turned, fields_in, mask_in, place_in, sem,
):
    local = []
    for i, ref in enumerate((precip, pet, soil_init, ksat)):
        local.append(pltpu.make_async_copy(ref, fields_in.at[i], sem.at[i]))
    local.append(pltpu.make_async_copy(land_mask, mask_in, sem.at[4]))
    local.append(pltpu.make_async_copy(places, place_in, sem.at[5]))
    for c in local:
        c.start()
    for c in local:
        c.wait()
    mask = mask_in[...].astype(F32)
    p = fields_in[0]
    s0 = fields_in[2]
    k = fields_in[3]
    wet = 2.0 * s0
    cap = k * (1.0 - wet)
    runoff = mask * p * p / (p + cap)
    wet2 = wet * wet
    drainage = 0.25 * mask * k * (wet2 * wet2)
    evap = mask * fields_in[1] * wet
    soil_out[...] = s0 + 0.1 * (mask * p - runoff - drainage - evap)
    rows = p.shape[1]
    fields = jnp.concatenate([runoff, drainage], axis=0)
    turned[0:8, :] = jnp.zeros((8, LANES), F32)
    turned[rows + 8 : rows + 16, :] = jnp.zeros((8, LANES), F32)
    turned[8 : rows + 8, :] = jnp.concatenate([fields] * 4, axis=0).T
    group = iota((32, LANES), 1) // 32
    for j in range(3):
        chunk = None
        for q in range(4):
            part = turned[pl.ds(6 + 4 * j + q, 32, stride=8), :]
            chunk = part if q == 0 else jnp.where(group == q, part, chunk)
        msg[pl.ds(j, 32, stride=4), :] = chunk
    place = place_in[...].astype(F32)
    msg[pl.ds(3, 16, stride=8), :] = place
    msg[pl.ds(7, 16, stride=8), :] = pltpu.roll(place, 64, 1)


def edge_kernel(head, sub, conduct, drain, code, top, bottom, code_edge, sem):
    copies = []
    for i, ref in enumerate((head, sub, conduct, drain, code)):
        into = slice(HALO * i, HALO * i + HALO)
        to_top = code_edge.at[0] if i == 4 else top.at[into, :]
        to_bottom = code_edge.at[1] if i == 4 else bottom.at[into, :]
        copies.append(pltpu.make_async_copy(ref.at[0:HALO, :], to_top, sem.at[2 * i]))
        copies.append(
            pltpu.make_async_copy(ref.at[OWN - HALO : OWN, :], to_bottom, sem.at[2 * i + 1])
        )
    for c in reversed(copies):
        c.start()
    for c in copies[8:]:
        c.wait()
    top[4 * HALO :, :] = code_edge[0].astype(F32)
    bottom[4 * HALO :, :] = code_edge[1].astype(F32)
    for c in copies[:8]:
        c.wait()


def spread_kernel(land, head_init, sub_init, conduct, drain, code, fine_out, turned):
    width = fine_out.shape[1]
    data = jnp.concatenate([land[pl.ds(j, 32, stride=4), :] for j in range(3)], axis=1)
    a, b, c = split3(data)
    turned[...] = jnp.concatenate([a, b, c, jnp.zeros_like(a)], axis=0).T
    lhs = jnp.concatenate([turned[pl.ds(q, 24, stride=16), :] for q in range(16)], axis=0)
    lhs = lhs.astype(BF16)
    src = iota((LANES, 256), 0)
    dst = iota((LANES, 256), 1)
    col = (iota((24, 256), 1) & 63) >> 2
    for n in range(width // 256):
        hot = ((src & 31) == ((dst + 256 * n) >> 6)) & (src < 96)
        spread = jnp.dot(lhs, jnp.where(hot, 1.0, 0.0).astype(BF16), preferred_element_type=F32)
        fine = spread[0:24]
        for q in range(1, 16):
            fine = jnp.where(col == q, spread[24 * q : 24 * q + 24], fine)
        fine_out[:, 256 * n : 256 * n + 256] = fine


def route_kernel(
    land, head_init, sub_init, conduct, drain, code, above, below, share, slot,
    head_out, sub_out, msg,
    h_a, h_b, s_a, s_b, g_w, a_w, dn_w, up_w, rt_w, lf_w, kp_w,
    head, sub, shares, slots, parts, sem,
):
    tiles = g_w.shape[0]
    width = tiles * LANES
    zero = jnp.zeros((ROWS, LANES), F32)
    share_copy = pltpu.make_async_copy(share, shares, sem.at[0])
    slot_copy = pltpu.make_async_copy(slot, slots, sem.at[3])
    share_copy.start()
    slot_copy.start()

    def window(own, field, j):
        lo = 8 * field
        at = cut(j)
        return jnp.concatenate(
            [above[lo : lo + 8, at], own[:, at].astype(F32), below[lo : lo + 8, at]], axis=0
        )

    for j in range(tiles):
        g_w[j] = window(conduct, 2, j)
        d = window(drain, 3, j)
        k = window(code, 4, j)
        moves = [jnp.where(k == float(i), d, 0.0) for i in range(4)]
        dn_w[j], up_w[j], rt_w[j], lf_w[j] = moves
        kp_w[j] = 1.0 - (moves[0] + moves[1] + moves[2] + moves[3])
    for j in range(tiles):
        g = g_w[j]
        left = pltpu.roll(g_w[j - 1], 1, 1) if j > 0 else zero
        right = pltpu.roll(g_w[j + 1], LANES - 1, 1) if j < tiles - 1 else zero
        total = pltpu.roll(g, 1, 0) + pltpu.roll(g, ROWS - 1, 0)
        total = total + left_of(pltpu.roll(g, 1, 1), left)
        total = total + right_of(pltpu.roll(g, LANES - 1, 1), right)
        a_w[j] = 1.0 - g * total

    low_half = iota((8, 256), 0) < 4
    for n in range(width // 256):
        fine = land[:, 256 * n : 256 * n + 256]
        for i in range(ROWS // 8):
            here = slice(8 * i, 8 * i + 8)
            at = slice(256 * n, 256 * n + 256)
            if i == 0:
                h0, s0 = above[0:8, at], above[8:16, at]
            elif i == ROWS // 8 - 1:
                h0, s0 = below[0:8, at], below[8:16, at]
            else:
                rows = slice(8 * i - 8, 8 * i)
                h0, s0 = head_init[rows, at], sub_init[rows, at]
            r = 4 * i
            h0 = h0 + jnp.where(low_half, fine[r : r + 1], fine[r + 2 : r + 3])
            s0 = s0 + jnp.where(low_half, fine[r + 1 : r + 2], fine[r + 3 : r + 4])
            for u in range(2):
                j = 2 * n + u
                h_a[j, here, :] = h0[:, cut(u)]
                s_a[j, here, :] = s0[:, cut(u)]

    def products(j, h_in, s_in):
        p = g_w[j] * h_in[j]
        s = s_in[j]
        return (
            p,
            pltpu.roll(p, 1, 1),
            pltpu.roll(p, LANES - 1, 1),
            pltpu.roll(rt_w[j] * s, 1, 1),
            pltpu.roll(lf_w[j] * s, LANES - 1, 1),
        )

    def substep(h_in, s_in, h_to, s_to):
        before = (zero,) * 5
        now = products(0, h_in, s_in)
        for j in range(tiles):
            after = products(j + 1, h_in, s_in) if j < tiles - 1 else (zero,) * 5
            p = now[0]
            s = s_in[j]
            flux = pltpu.roll(p, 1, 0) + pltpu.roll(p, ROWS - 1, 0)
            flux = flux + left_of(now[1], before[1])
            flux = flux + right_of(now[2], after[2])
            h_to[j] = a_w[j] * h_in[j] + g_w[j] * flux
            new = pltpu.roll(dn_w[j] * s, 1, 0) + pltpu.roll(up_w[j] * s, ROWS - 1, 0)
            new = new + kp_w[j] * s
            new = new + left_of(now[3], before[3])
            s_to[j] = new + right_of(now[4], after[4])
            before, now = now, after

    for i in range(ITERS // 2):
        substep(h_a, s_a, h_b, s_b)
        substep(h_b, s_b, h_a, s_a)

    share_copy.wait()
    slot_copy.wait()
    for j in range(tiles):
        at = cut(j)
        h = h_a[j, HALO : HALO + OWN, :]
        sub[:, at] = s_a[j, HALO : HALO + OWN, :]
        inflow = shares[:, at] * h
        head[:, at] = h - inflow
        parts[0, :, at], parts[1, :, at], parts[2, :, at] = split3(inflow)
        q = slots[:, at]
        parts[3, :, at] = (q >> 6).astype(F32)
        parts[4, :, at] = (q & 63).astype(F32)
    head_copy = pltpu.make_async_copy(head, head_out, sem.at[1])
    sub_copy = pltpu.make_async_copy(sub, sub_out, sem.at[2])
    head_copy.start()
    sub_copy.start()

    owner = iota((32, width), 0).astype(F32).astype(BF16)
    place = iota((64, width), 0).astype(F32).astype(BF16)
    one = jnp.ones((64, width), BF16)
    none64 = jnp.zeros((64, width), BF16)
    none32 = jnp.zeros((32, width), BF16)

    def wide(row, n):
        return jnp.broadcast_to(row, (n, width)).astype(BF16)

    total = jnp.zeros((96, 64), F32)
    for r in range(OWN):
        at = slice(r, r + 1)
        hi = wide(parts[3, at, :], 32) == owner
        lhs = jnp.concatenate(
            [jnp.where(hi, wide(parts[i, at, :], 32), none32) for i in range(3)], axis=0
        )
        rhs = jnp.where(wide(parts[4, at, :], 64) == place, one, none64)
        total = total + lax.dot_general(
            lhs, rhs, (((1,), (1,)), ((), ())), preferred_element_type=F32
        )
    total = total[0:32] + total[32:64] + total[64:96]
    msg[...] = jnp.concatenate([total, jnp.zeros_like(total)], axis=1)
    head_copy.wait()
    sub_copy.wait()


def reach_kernel(land, got, out):
    low = iota((16, LANES), 1) < 64

    def pack(x):
        return jnp.where(low, x[0:16], pltpu.roll(x[16:32], 64, 1))

    sums = pack(got[...])
    place = pack(land[pl.ds(3, 32, stride=4), :]).astype(jnp.int32)

    def line(x):
        return jnp.concatenate([x[u : u + 1] for u in range(16)], axis=1)

    width = 16 * LANES
    hi = line((place >> 7).astype(F32)) == iota((16, width), 0).astype(F32)
    lhs = jnp.concatenate([jnp.where(hi, line(x), 0.0) for x in split3(sums)], axis=0)
    lo = line((place & 127).astype(F32)) == iota((LANES, width), 0).astype(F32)
    total = lax.dot_general(
        lhs.astype(BF16), jnp.where(lo, 1.0, 0.0).astype(BF16),
        (((1,), (1,)), ((), ())), preferred_element_type=F32,
    )
    out[...] = total[0:16] + total[16:32] + total[32:48]


def local(
    precip,
    pet,
    soil_init,
    ksat,
    land_mask,
    head_init,
    subsurface_init,
    conduct,
    drain_rate,
    flow_code,
    channel_share,
    cell_slot,
    slot_reach,
):
    vmem = pl.BlockSpec(memory_space=pltpu.VMEM)
    far = pl.BlockSpec(memory_space=pltpu.HBM)
    peers = lax.axis_size("tile")
    width = head_init.shape[1]
    tiles = width // LANES

    def hbm(x):
        return pltpu.with_memory_space_constraint(x, pltpu.HBM)

    def array(*shape):
        return jax.ShapeDtypeStruct(shape, F32)

    soil, msg = pl.pallas_call(
        land_kernel,
        out_shape=(array(*precip.shape), array(4 * peers, LANES)),
        in_specs=[far] * 6,
        out_specs=(vmem,) * 2,
        scratch_shapes=[
            pltpu.VMEM((precip.shape[1] + 16, LANES), F32),
            pltpu.VMEM((4,) + precip.shape, F32),
            pltpu.VMEM(precip.shape, jnp.int32),
            pltpu.VMEM((16, LANES), jnp.int32),
            pltpu.SemaphoreType.DMA((6,)),
        ],
        compiler_params=pltpu.CompilerParams(vmem_limit_bytes=6 * MIB),
        name="land_step",
    )(*map(hbm, (precip, pet, soil_init, ksat, land_mask, slot_reach.reshape(-1, LANES))))
    grid = (head_init, subsurface_init, conduct, drain_rate, flow_code)
    top, bottom = pl.pallas_call(
        edge_kernel,
        out_shape=(array(5 * HALO, width),) * 2,
        in_specs=[far] * 5,
        out_specs=(vmem,) * 2,
        scratch_shapes=[
            pltpu.VMEM((2, HALO, width), jnp.int32),
            pltpu.SemaphoreType.DMA((10,)),
        ],
        compiler_params=pltpu.CompilerParams(vmem_limit_bytes=6 * MIB),
        name="edges",
    )(*map(hbm, grid))
    up = [(i, i + 1) for i in range(peers - 1)]
    down = [(j, i) for i, j in up]
    above = lax.ppermute(bottom, "tile", up)
    below = lax.ppermute(top, "tile", down)
    land = lax.all_to_all(
        msg.reshape(peers, 4, LANES), "tile", split_axis=0, concat_axis=0, tiled=True
    ).reshape(4 * peers, LANES)

    fine = pl.pallas_call(
        spread_kernel,
        out_shape=array(24, width),
        in_specs=[vmem] * 6,
        out_specs=vmem,
        scratch_shapes=[pltpu.VMEM((384, LANES), F32)],
        compiler_params=pltpu.CompilerParams(vmem_limit_bytes=8 * MIB),
        cost_estimate=pl.CostEstimate(flops=4*10**9, transcendentals=0, bytes_accessed=1 << 18),
        name="spread",
    )(land, *grid)

    window = pltpu.VMEM((tiles, ROWS, LANES), F32)
    plane = pltpu.VMEM((OWN, width), F32)
    head, sub, sums = pl.pallas_call(
        route_kernel,
        out_shape=(array(OWN, width), array(OWN, width), array(peers, LANES)),
        in_specs=[vmem] * 8 + [far] * 2,
        out_specs=(far, far, vmem),
        scratch_shapes=[window] * 11
        + [plane] * 3
        + [pltpu.VMEM((OWN, width), jnp.int32), pltpu.VMEM((5, OWN, width), F32)]
        + [pltpu.SemaphoreType.DMA((4,))],
        compiler_params=pltpu.CompilerParams(vmem_limit_bytes=16 * MIB),
        name="route",
    )(fine, *grid, above, below, hbm(channel_share), hbm(cell_slot))
    sums = lax.all_to_all(sums, "tile", split_axis=0, concat_axis=0, tiled=True)
    reach = pl.pallas_call(
        reach_kernel,
        out_shape=array(16, LANES),
        in_specs=[vmem] * 2,
        out_specs=vmem,
        compiler_params=pltpu.CompilerParams(vmem_limit_bytes=6 * MIB),
        name="reach_sums",
    )(land, sums)
    return (soil, head, sub, reach.reshape(-1))


def solution(mesh):
    rows = P(("member", "tile"), None)
    flat = P(("member", "tile"))
    return jax.shard_map(
        local,
        mesh=mesh,
        in_specs=(rows,) * 12 + (flat,),
        out_specs=(rows, rows, rows, flat),
        check_vma=False,
    )
```

```python
import jax
import jax.numpy as jnp
from jax import lax
from jax.experimental import pallas as pl
from jax.experimental.pallas import tpu as pltpu
from jax.sharding import PartitionSpec as P

ITERS = 6
HALO = 8
OWN = 32
ROWS = OWN + 2 * HALO
LANES = 128
F32 = jnp.float32
BF16 = jnp.bfloat16
MIB = 1024 * 1024


def iota(shape, dim):
    return lax.broadcasted_iota(jnp.int32, shape, dim)


def split3(x):
    a = x.astype(BF16).astype(F32)
    r = x - a
    b = r.astype(BF16).astype(F32)
    return a, b, r - b


def cut(j):
    return slice(LANES * j, LANES * (j + 1))


def left_of(tile, before):
    return jnp.where(iota(tile.shape, 1) == 0, before, tile)


def right_of(tile, after):
    return jnp.where(iota(tile.shape, 1) == LANES - 1, after, tile)


def send_kernel(
    precip, pet, soil_init, ksat, land_mask, places, head, sub, conduct, drain, code,
    soil_out, msg, near, far, turned, fields_in, mask_in, place_in, code_edge, sem,
):
    local = []
    for i, ref in enumerate((precip, pet, soil_init, ksat)):
        local.append(pltpu.make_async_copy(ref, fields_in.at[i], sem.at[10 + i]))
    local.append(pltpu.make_async_copy(land_mask, mask_in, sem.at[14]))
    local.append(pltpu.make_async_copy(places, place_in, sem.at[15]))
    odd = lax.axis_index("tile") & 1
    near_rows = pl.ds(pl.multiple_of((1 - odd) * (OWN - HALO), HALO), HALO)
    far_rows = pl.ds(pl.multiple_of(odd * (OWN - HALO), HALO), HALO)
    copies = []
    for i, ref in enumerate((head, sub, conduct, drain)):
        into = slice(HALO * i, HALO * i + HALO)
        copies.append(pltpu.make_async_copy(ref.at[near_rows, :], near.at[into, :], sem.at[2 * i]))
        copies.append(pltpu.make_async_copy(ref.at[far_rows, :], far.at[into, :], sem.at[2 * i + 1]))
    codes = (
        pltpu.make_async_copy(code.at[near_rows, :], code_edge.at[0], sem.at[8]),
        pltpu.make_async_copy(code.at[far_rows, :], code_edge.at[1], sem.at[9]),
    )
    for c in local:
        c.start()
    for c in codes:
        c.start()
    for c in copies:
        c.start()
    for c in local:
        c.wait()
    mask = mask_in[...].astype(F32)
    p = fields_in[0]
    s0 = fields_in[2]
    k = fields_in[3]
    wet = 2.0 * s0
    cap = k * (1.0 - wet)
    runoff = mask * p * p / (p + cap)
    wet2 = wet * wet
    drainage = 0.25 * mask * k * (wet2 * wet2)
    evap = mask * fields_in[1] * wet
    soil_out[...] = s0 + 0.1 * (mask * p - runoff - drainage - evap)
    rows = p.shape[1]
    fields = jnp.concatenate([runoff, drainage], axis=0)
    turned[0:8, :] = jnp.zeros((8, LANES), F32)
    turned[rows + 8 : rows + 16, :] = jnp.zeros((8, LANES), F32)
    turned[8 : rows + 8, :] = jnp.concatenate([fields] * 4, axis=0).T
    group = iota((32, LANES), 1) // 32
    for j in range(3):
        chunk = None
        for q in range(4):
            part = turned[pl.ds(6 + 4 * j + q, 32, stride=8), :]
            chunk = part if q == 0 else jnp.where(group == q, part, chunk)
        msg[pl.ds(j, 32, stride=4), :] = chunk
    place = place_in[...].astype(F32)
    msg[pl.ds(3, 16, stride=8), :] = place
    msg[pl.ds(7, 16, stride=8), :] = pltpu.roll(place, 64, 1)
    for c in codes:
        c.wait()
    near[4 * HALO :, :] = code_edge[0].astype(F32)
    far[4 * HALO :, :] = code_edge[1].astype(F32)
    for c in copies:
        c.wait()


def route_kernel(
    land, head_init, sub_init, conduct, drain, code, near, far, share, slot,
    head_out, sub_out, msg,
    turned, h_a, h_b, s_a, s_b, g_w, a_w, dn_w, up_w, rt_w, lf_w, kp_w,
    head, sub, shares, slots, parts, sem,
):
    tiles = g_w.shape[0]
    width = tiles * LANES
    zero = jnp.zeros((ROWS, LANES), F32)
    share_copy = pltpu.make_async_copy(share, shares, sem.at[0])
    slot_copy = pltpu.make_async_copy(slot, slots, sem.at[3])
    share_copy.start()
    slot_copy.start()

    odd = (lax.axis_index("tile") & 1) == 1

    def above(field, at):
        rows = slice(HALO * field, HALO * field + HALO)
        return jnp.where(odd, near[rows, at], far[rows, at])

    def below(field, at):
        rows = slice(HALO * field, HALO * field + HALO)
        return jnp.where(odd, far[rows, at], near[rows, at])

    def window(own, field, j):
        at = cut(j)
        return jnp.concatenate(
            [above(field, at), own[:, at].astype(F32), below(field, at)], axis=0
        )

    for j in range(tiles):
        g_w[j] = window(conduct, 2, j)
        d = window(drain, 3, j)
        k = window(code, 4, j)
        moves = [jnp.where(k == float(i), d, 0.0) for i in range(4)]
        dn_w[j], up_w[j], rt_w[j], lf_w[j] = moves
        kp_w[j] = 1.0 - (moves[0] + moves[1] + moves[2] + moves[3])
    for j in range(tiles):
        g = g_w[j]
        left = pltpu.roll(g_w[j - 1], 1, 1) if j > 0 else zero
        right = pltpu.roll(g_w[j + 1], LANES - 1, 1) if j < tiles - 1 else zero
        total = pltpu.roll(g, 1, 0) + pltpu.roll(g, ROWS - 1, 0)
        total = total + left_of(pltpu.roll(g, 1, 1), left)
        total = total + right_of(pltpu.roll(g, LANES - 1, 1), right)
        a_w[j] = 1.0 - g * total

    data = jnp.concatenate([land[pl.ds(j, 32, stride=4), :] for j in range(3)], axis=1)
    a, b, c = split3(data)
    turned[...] = jnp.concatenate([a, b, c, jnp.zeros_like(a)], axis=0).T
    lhs = jnp.concatenate([turned[pl.ds(q, 24, stride=16), :] for q in range(16)], axis=0)
    lhs = lhs.astype(BF16)
    low_half = iota((8, 256), 0) < 4
    src = iota((LANES, 256), 0)
    dst = iota((LANES, 256), 1)
    col = (iota((24, 256), 1) & 63) >> 2
    for n in range(width // 256):
        hot = ((src & 31) == ((dst + 256 * n) >> 6)) & (src < 96)
        spread = jnp.dot(lhs, jnp.where(hot, 1.0, 0.0).astype(BF16), preferred_element_type=F32)
        fine = spread[0:24]
        for q in range(1, 16):
            fine = jnp.where(col == q, spread[24 * q : 24 * q + 24], fine)
        for i in range(ROWS // 8):
            here = slice(8 * i, 8 * i + 8)
            at = slice(256 * n, 256 * n + 256)
            if i == 0:
                h0, s0 = above(0, at), above(1, at)
            elif i == ROWS // 8 - 1:
                h0, s0 = below(0, at), below(1, at)
            else:
                rows = slice(8 * i - 8, 8 * i)
                h0, s0 = head_init[rows, at], sub_init[rows, at]
            r = 4 * i
            h0 = h0 + jnp.where(low_half, fine[r : r + 1], fine[r + 2 : r + 3])
            s0 = s0 + jnp.where(low_half, fine[r + 1 : r + 2], fine[r + 3 : r + 4])
            for u in range(2):
                j = 2 * n + u
                h_a[j, here, :] = h0[:, cut(u)]
                s_a[j, here, :] = s0[:, cut(u)]

    def products(j, h_in, s_in):
        p = g_w[j] * h_in[j]
        s = s_in[j]
        return (
            p,
            pltpu.roll(p, 1, 1),
            pltpu.roll(p, LANES - 1, 1),
            pltpu.roll(rt_w[j] * s, 1, 1),
            pltpu.roll(lf_w[j] * s, LANES - 1, 1),
        )

    def substep(h_in, s_in, h_to, s_to):
        before = (zero,) * 5
        now = products(0, h_in, s_in)
        for j in range(tiles):
            after = products(j + 1, h_in, s_in) if j < tiles - 1 else (zero,) * 5
            p = now[0]
            s = s_in[j]
            flux = pltpu.roll(p, 1, 0) + pltpu.roll(p, ROWS - 1, 0)
            flux = flux + left_of(now[1], before[1])
            flux = flux + right_of(now[2], after[2])
            h_to[j] = a_w[j] * h_in[j] + g_w[j] * flux
            new = pltpu.roll(dn_w[j] * s, 1, 0) + pltpu.roll(up_w[j] * s, ROWS - 1, 0)
            new = new + kp_w[j] * s
            new = new + left_of(now[3], before[3])
            s_to[j] = new + right_of(now[4], after[4])
            before, now = now, after

    for i in range(ITERS // 2):
        substep(h_a, s_a, h_b, s_b)
        substep(h_b, s_b, h_a, s_a)

    share_copy.wait()
    slot_copy.wait()
    for j in range(tiles):
        at = cut(j)
        h = h_a[j, HALO : HALO + OWN, :]
        sub[:, at] = s_a[j, HALO : HALO + OWN, :]
        inflow = shares[:, at] * h
        head[:, at] = h - inflow
        parts[0, :, at], parts[1, :, at], parts[2, :, at] = split3(inflow)
        q = slots[:, at]
        parts[3, :, at] = (q >> 6).astype(F32)
        parts[4, :, at] = (q & 63).astype(F32)
    head_copy = pltpu.make_async_copy(head, head_out, sem.at[1])
    sub_copy = pltpu.make_async_copy(sub, sub_out, sem.at[2])
    head_copy.start()
    sub_copy.start()

    owner = iota((32, width), 0).astype(F32).astype(BF16)
    place = iota((64, width), 0).astype(F32).astype(BF16)
    one = jnp.ones((64, width), BF16)
    none64 = jnp.zeros((64, width), BF16)
    none32 = jnp.zeros((32, width), BF16)

    def wide(row, n):
        return jnp.broadcast_to(row, (n, width)).astype(BF16)

    total = jnp.zeros((96, 64), F32)
    for r in range(OWN):
        at = slice(r, r + 1)
        hi = wide(parts[3, at, :], 32) == owner
        lhs = jnp.concatenate(
            [jnp.where(hi, wide(parts[i, at, :], 32), none32) for i in range(3)], axis=0
        )
        rhs = jnp.where(wide(parts[4, at, :], 64) == place, one, none64)
        total = total + lax.dot_general(
            lhs, rhs, (((1,), (1,)), ((), ())), preferred_element_type=F32
        )
    total = total[0:32] + total[32:64] + total[64:96]
    msg[...] = jnp.concatenate([total, jnp.zeros_like(total)], axis=1)
    head_copy.wait()
    sub_copy.wait()


def reach_kernel(land, got, out):
    low = iota((16, LANES), 1) < 64

    def pack(x):
        return jnp.where(low, x[0:16], pltpu.roll(x[16:32], 64, 1))

    sums = pack(got[...])
    place = pack(land[pl.ds(3, 32, stride=4), :]).astype(jnp.int32)

    def line(x):
        return jnp.concatenate([x[u : u + 1] for u in range(16)], axis=1)

    width = 16 * LANES
    hi = line((place >> 7).astype(F32)) == iota((16, width), 0).astype(F32)
    lhs = jnp.concatenate([jnp.where(hi, line(x), 0.0) for x in split3(sums)], axis=0)
    lo = line((place & 127).astype(F32)) == iota((LANES, width), 0).astype(F32)
    total = lax.dot_general(
        lhs.astype(BF16), jnp.where(lo, 1.0, 0.0).astype(BF16),
        (((1,), (1,)), ((), ())), preferred_element_type=F32,
    )
    out[...] = total[0:16] + total[16:32] + total[32:48]


def local(
    precip,
    pet,
    soil_init,
    ksat,
    land_mask,
    head_init,
    subsurface_init,
    conduct,
    drain_rate,
    flow_code,
    channel_share,
    cell_slot,
    slot_reach,
):
    vmem = pl.BlockSpec(memory_space=pltpu.VMEM)
    outside = pl.BlockSpec(memory_space=pltpu.HBM)
    peers = lax.axis_size("tile")
    width = head_init.shape[1]
    tiles = width // LANES

    def hbm(x):
        return pltpu.with_memory_space_constraint(x, pltpu.HBM)

    def array(*shape):
        return jax.ShapeDtypeStruct(shape, F32)

    soil, msg, near, far = pl.pallas_call(
        send_kernel,
        out_shape=(
            array(*precip.shape), array(4 * peers, LANES), array(40, width), array(40, width),
        ),
        in_specs=[outside] * 11,
        out_specs=(vmem,) * 4,
        scratch_shapes=[
            pltpu.VMEM((precip.shape[1] + 16, LANES), F32),
            pltpu.VMEM((4,) + precip.shape, F32),
            pltpu.VMEM(precip.shape, jnp.int32),
            pltpu.VMEM((16, LANES), jnp.int32),
            pltpu.VMEM((2, 8, width), jnp.int32),
            pltpu.SemaphoreType.DMA((16,)),
        ],
        compiler_params=pltpu.CompilerParams(vmem_limit_bytes=6 * MIB),
        name="send",
    )(
        *map(
            hbm,
            (
                precip, pet, soil_init, ksat, land_mask, slot_reach.reshape(-1, LANES),
                head_init, subsurface_init, conduct, drain_rate, flow_code,
            ),
        )
    )
    near = lax.ppermute(near, "tile", [(i, i ^ 1) for i in range(peers)])
    far = lax.ppermute(far, "tile", [(i, ((i + 1) ^ 1) - 1) for i in range(1, peers - 1)])
    land = lax.all_to_all(
        msg.reshape(peers, 4, LANES), "tile", split_axis=0, concat_axis=0, tiled=True
    ).reshape(4 * peers, LANES)

    window = pltpu.VMEM((tiles, ROWS, LANES), F32)
    plane = pltpu.VMEM((OWN, width), F32)
    head, sub, sums = pl.pallas_call(
        route_kernel,
        out_shape=(array(OWN, width), array(OWN, width), array(peers, LANES)),
        in_specs=[vmem] * 8 + [outside] * 2,
        out_specs=(outside, outside, vmem),
        scratch_shapes=[pltpu.VMEM((384, LANES), F32)]
        + [window] * 11
        + [plane] * 3
        + [pltpu.VMEM((OWN, width), jnp.int32), pltpu.VMEM((5, OWN, width), F32)]
        + [pltpu.SemaphoreType.DMA((4,))],
        compiler_params=pltpu.CompilerParams(vmem_limit_bytes=16 * MIB),
        name="route",
    )(
        land, head_init, subsurface_init, conduct, drain_rate, flow_code, near, far,
        hbm(channel_share), hbm(cell_slot),
    )
    sums = lax.all_to_all(sums, "tile", split_axis=0, concat_axis=0, tiled=True)
    reach = pl.pallas_call(
        reach_kernel,
        out_shape=array(16, LANES),
        in_specs=[vmem] * 2,
        out_specs=vmem,
        compiler_params=pltpu.CompilerParams(vmem_limit_bytes=6 * MIB),
        name="reach_sums",
    )(land, sums)
    return (soil, head, sub, reach.reshape(-1))


def solution(mesh):
    rows = P(("member", "tile"), None)
    flat = P(("member", "tile"))
    return jax.shard_map(
        local,
        mesh=mesh,
        in_specs=(rows,) * 12 + (flat,),
        out_specs=(rows, rows, rows, flat),
        check_vma=False,
    )
```

```python
import jax
import jax.numpy as jnp
from jax import lax
from jax.experimental import pallas as pl
from jax.experimental.pallas import tpu as pltpu
from jax.sharding import PartitionSpec as P

ITERS = 6
HALO = 8
OWN = 32
ROWS = OWN + 2 * HALO
LANES = 128
F32 = jnp.float32
BF16 = jnp.bfloat16
MIB = 1024 * 1024


def iota(shape, dim):
    return lax.broadcasted_iota(jnp.int32, shape, dim)


def split3(x):
    a = x.astype(BF16).astype(F32)
    r = x - a
    b = r.astype(BF16).astype(F32)
    return a, b, r - b


def cut(j):
    return slice(LANES * j, LANES * (j + 1))


def left_of(tile, before):
    return jnp.where(iota(tile.shape, 1) == 0, before, tile)


def right_of(tile, after):
    return jnp.where(iota(tile.shape, 1) == LANES - 1, after, tile)


def send_kernel(
    precip, pet, soil_init, ksat, land_mask, places, head, sub, conduct, drain, code,
    soil_out, msg, near, far, turned, fields_in, mask_in, place_in, code_edge, sem,
):
    local = []
    for i, ref in enumerate((precip, pet, soil_init, ksat)):
        local.append(pltpu.make_async_copy(ref, fields_in.at[i], sem.at[10 + i]))
    local.append(pltpu.make_async_copy(land_mask, mask_in, sem.at[14]))
    local.append(pltpu.make_async_copy(places, place_in, sem.at[15]))
    odd = lax.axis_index("tile") & 1
    near_rows = pl.ds(pl.multiple_of((1 - odd) * (OWN - HALO), HALO), HALO)
    far_rows = pl.ds(pl.multiple_of(odd * (OWN - HALO), HALO), HALO)
    copies = []
    for i, ref in enumerate((head, sub, conduct, drain)):
        into = slice(HALO * i, HALO * i + HALO)
        copies.append(pltpu.make_async_copy(ref.at[near_rows, :], near.at[into, :], sem.at[2 * i]))
        copies.append(pltpu.make_async_copy(ref.at[far_rows, :], far.at[into, :], sem.at[2 * i + 1]))
    codes = (
        pltpu.make_async_copy(code.at[near_rows, :], code_edge.at[0], sem.at[8]),
        pltpu.make_async_copy(code.at[far_rows, :], code_edge.at[1], sem.at[9]),
    )
    for c in local:
        c.start()
    for c in codes:
        c.start()
    for c in copies:
        c.start()
    for c in local:
        c.wait()
    mask = mask_in[...].astype(F32)
    p = fields_in[0]
    s0 = fields_in[2]
    k = fields_in[3]
    wet = 2.0 * s0
    cap = k * (1.0 - wet)
    runoff = mask * p * p / (p + cap)
    wet2 = wet * wet
    drainage = 0.25 * mask * k * (wet2 * wet2)
    evap = mask * fields_in[1] * wet
    soil_out[...] = s0 + 0.1 * (mask * p - runoff - drainage - evap)
    rows = p.shape[1]
    fields = jnp.concatenate([runoff, drainage], axis=0)
    turned[0:8, :] = jnp.zeros((8, LANES), F32)
    turned[rows + 8 : rows + 16, :] = jnp.zeros((8, LANES), F32)
    turned[8 : rows + 8, :] = jnp.concatenate([fields] * 4, axis=0).T
    group = iota((32, LANES), 1) // 32
    for j in range(3):
        chunk = None
        for q in range(4):
            part = turned[pl.ds(6 + 4 * j + q, 32, stride=8), :]
            chunk = part if q == 0 else jnp.where(group == q, part, chunk)
        msg[pl.ds(j, 32, stride=4), :] = chunk
    place = place_in[...].astype(F32)
    msg[pl.ds(3, 16, stride=8), :] = place
    msg[pl.ds(7, 16, stride=8), :] = pltpu.roll(place, 64, 1)
    for c in codes:
        c.wait()
    near[4 * HALO :, :] = code_edge[0].astype(F32)
    far[4 * HALO :, :] = code_edge[1].astype(F32)
    for c in copies:
        c.wait()


def route_kernel(
    land, head_init, sub_init, conduct, drain, code, near, far, share, slot,
    head_out, sub_out, msg,
    turned, h_a, h_b, s_a, s_b, g_w, a_w, dn_w, up_w, rt_w, lf_w, kp_w,
    head, sub, shares, slots, parts, sem,
):
    tiles = g_w.shape[0]
    width = tiles * LANES
    zero = jnp.zeros((ROWS, LANES), F32)
    share_copy = pltpu.make_async_copy(share, shares, sem.at[0])
    slot_copy = pltpu.make_async_copy(slot, slots, sem.at[3])
    share_copy.start()
    slot_copy.start()

    odd = (lax.axis_index("tile") & 1) == 1

    def above(field, at):
        rows = slice(HALO * field, HALO * field + HALO)
        return jnp.where(odd, near[rows, at], far[rows, at])

    def below(field, at):
        rows = slice(HALO * field, HALO * field + HALO)
        return jnp.where(odd, far[rows, at], near[rows, at])

    def window(own, field, j):
        at = cut(j)
        return jnp.concatenate(
            [above(field, at), own[:, at].astype(F32), below(field, at)], axis=0
        )

    for j in range(tiles):
        g_w[j] = window(conduct, 2, j)
        d = window(drain, 3, j)
        k = window(code, 4, j)
        moves = [jnp.where(k == float(i), d, 0.0) for i in range(4)]
        dn_w[j], up_w[j], rt_w[j], lf_w[j] = moves
        kp_w[j] = 1.0 - (moves[0] + moves[1] + moves[2] + moves[3])
    for j in range(tiles):
        g = g_w[j]
        left = pltpu.roll(g_w[j - 1], 1, 1) if j > 0 else zero
        right = pltpu.roll(g_w[j + 1], LANES - 1, 1) if j < tiles - 1 else zero
        total = pltpu.roll(g, 1, 0) + pltpu.roll(g, ROWS - 1, 0)
        total = total + left_of(pltpu.roll(g, 1, 1), left)
        total = total + right_of(pltpu.roll(g, LANES - 1, 1), right)
        a_w[j] = 1.0 - g * total

    data = jnp.concatenate([land[pl.ds(j, 32, stride=4), :] for j in range(3)], axis=1)
    a, b, c = split3(data)
    turned[...] = jnp.concatenate([a, b, c, jnp.zeros_like(a)], axis=0).T
    lhs = jnp.concatenate([turned[pl.ds(q, 24, stride=16), :] for q in range(16)], axis=0)
    lhs = lhs.astype(BF16)
    low_half = iota((8, 256), 0) < 4
    src = iota((LANES, 256), 0)
    dst = iota((LANES, 256), 1)
    col = (iota((24, 256), 1) & 63) >> 2
    for n in range(width // 256):
        hot = ((src & 31) == ((dst + 256 * n) >> 6)) & (src < 96)
        spread = jnp.dot(lhs, jnp.where(hot, 1.0, 0.0).astype(BF16), preferred_element_type=F32)
        fine = spread[0:24]
        for q in range(1, 16):
            fine = jnp.where(col == q, spread[24 * q : 24 * q + 24], fine)
        for i in range(ROWS // 8):
            here = slice(8 * i, 8 * i + 8)
            at = slice(256 * n, 256 * n + 256)
            if i == 0:
                h0, s0 = above(0, at), above(1, at)
            elif i == ROWS // 8 - 1:
                h0, s0 = below(0, at), below(1, at)
            else:
                rows = slice(8 * i - 8, 8 * i)
                h0, s0 = head_init[rows, at], sub_init[rows, at]
            r = 4 * i
            h0 = h0 + jnp.where(low_half, fine[r : r + 1], fine[r + 2 : r + 3])
            s0 = s0 + jnp.where(low_half, fine[r + 1 : r + 2], fine[r + 3 : r + 4])
            for u in range(2):
                j = 2 * n + u
                h_a[j, here, :] = h0[:, cut(u)]
                s_a[j, here, :] = s0[:, cut(u)]

    def products(j, h_in, s_in):
        p = g_w[j] * h_in[j]
        s = s_in[j]
        return (
            p,
            pltpu.roll(p, 1, 1),
            pltpu.roll(p, LANES - 1, 1),
            pltpu.roll(rt_w[j] * s, 1, 1),
            pltpu.roll(lf_w[j] * s, LANES - 1, 1),
        )

    def substep(h_in, s_in, keep, take):
        before = (zero,) * 5
        now = products(0, h_in, s_in)
        for j in range(tiles):
            after = products(j + 1, h_in, s_in) if j < tiles - 1 else (zero,) * 5
            p = now[0]
            s = s_in[j]
            flux = pltpu.roll(p, 1, 0) + pltpu.roll(p, ROWS - 1, 0)
            flux = flux + left_of(now[1], before[1])
            flux = flux + right_of(now[2], after[2])
            new = pltpu.roll(dn_w[j] * s, 1, 0) + pltpu.roll(up_w[j] * s, ROWS - 1, 0)
            new = new + left_of(now[3], before[3])
            new = new + right_of(now[4], after[4])
            h = a_w[j, keep, :] * h_in[j, keep, :] + g_w[j, keep, :] * flux[keep]
            take(j, h, new[keep] + kp_w[j, keep, :] * s[keep])
            before, now = now, after

    def store(h_to, s_to):
        def take(j, h, s):
            h_to[j] = h
            s_to[j] = s

        return take

    def finish(j, h, s):
        at = cut(j)
        sub[:, at] = s
        inflow = shares[:, at] * h
        head[:, at] = h - inflow
        coarse = inflow.astype(BF16).astype(F32)
        parts[0, :, at] = coarse
        parts[1, :, at] = inflow - coarse
        q = slots[:, at]
        parts[2, :, at] = (q >> 6).astype(F32)
        parts[3, :, at] = (q & 63).astype(F32)

    source = (h_a, s_a)
    target = (h_b, s_b)
    for i in range(ITERS - 1):
        substep(*source, slice(0, ROWS), store(*target))
        source, target = target, source
    share_copy.wait()
    slot_copy.wait()
    substep(*source, slice(HALO, HALO + OWN), finish)
    head_copy = pltpu.make_async_copy(head, head_out, sem.at[1])
    sub_copy = pltpu.make_async_copy(sub, sub_out, sem.at[2])
    head_copy.start()
    sub_copy.start()

    owner = iota((32, width), 0).astype(F32).astype(BF16)
    place = iota((64, width), 0).astype(F32).astype(BF16)
    one = jnp.ones((64, width), BF16)
    none = jnp.zeros((64, width), BF16)

    def wide(i, r, n):
        return jnp.broadcast_to(parts[i, r : r + 1, :], (n, width)).astype(BF16)

    total = jnp.zeros((64, 64), F32)
    for r in range(OWN):
        hi = wide(2, r, 32) == owner
        lhs = jnp.concatenate([jnp.where(hi, wide(i, r, 32), none[0:32]) for i in range(2)], axis=0)
        rhs = jnp.where(wide(3, r, 64) == place, one, none)
        total = total + lax.dot_general(
            lhs, rhs, (((1,), (1,)), ((), ())), preferred_element_type=F32
        )
    total = total[0:32] + total[32:64]
    msg[...] = jnp.concatenate([total, jnp.zeros_like(total)], axis=1)
    head_copy.wait()
    sub_copy.wait()


def reach_kernel(land, got, out):
    low = iota((16, LANES), 1) < 64

    def pack(x):
        return jnp.where(low, x[0:16], pltpu.roll(x[16:32], 64, 1))

    sums = pack(got[...])
    place = pack(land[pl.ds(3, 32, stride=4), :]).astype(jnp.int32)

    def line(x):
        return jnp.concatenate([x[u : u + 1] for u in range(16)], axis=1)

    width = 16 * LANES
    hi = line((place >> 7).astype(F32)) == iota((16, width), 0).astype(F32)
    lhs = jnp.concatenate([jnp.where(hi, line(x), 0.0) for x in split3(sums)], axis=0)
    lo = line((place & 127).astype(F32)) == iota((LANES, width), 0).astype(F32)
    total = lax.dot_general(
        lhs.astype(BF16), jnp.where(lo, 1.0, 0.0).astype(BF16),
        (((1,), (1,)), ((), ())), preferred_element_type=F32,
    )
    out[...] = total[0:16] + total[16:32] + total[32:48]


def local(
    precip,
    pet,
    soil_init,
    ksat,
    land_mask,
    head_init,
    subsurface_init,
    conduct,
    drain_rate,
    flow_code,
    channel_share,
    cell_slot,
    slot_reach,
):
    vmem = pl.BlockSpec(memory_space=pltpu.VMEM)
    outside = pl.BlockSpec(memory_space=pltpu.HBM)
    peers = lax.axis_size("tile")
    width = head_init.shape[1]
    tiles = width // LANES

    def hbm(x):
        return pltpu.with_memory_space_constraint(x, pltpu.HBM)

    def array(*shape):
        return jax.ShapeDtypeStruct(shape, F32)

    soil, msg, near, far = pl.pallas_call(
        send_kernel,
        out_shape=(
            array(*precip.shape), array(4 * peers, LANES), array(40, width), array(40, width),
        ),
        in_specs=[outside] * 11,
        out_specs=(vmem,) * 4,
        scratch_shapes=[
            pltpu.VMEM((precip.shape[1] + 16, LANES), F32),
            pltpu.VMEM((4,) + precip.shape, F32),
            pltpu.VMEM(precip.shape, jnp.int32),
            pltpu.VMEM((16, LANES), jnp.int32),
            pltpu.VMEM((2, 8, width), jnp.int32),
            pltpu.SemaphoreType.DMA((16,)),
        ],
        compiler_params=pltpu.CompilerParams(vmem_limit_bytes=6 * MIB),
        name="send",
    )(
        *map(
            hbm,
            (
                precip, pet, soil_init, ksat, land_mask, slot_reach.reshape(-1, LANES),
                head_init, subsurface_init, conduct, drain_rate, flow_code,
            ),
        )
    )
    near = lax.ppermute(near, "tile", [(i, i ^ 1) for i in range(peers)])
    far = lax.ppermute(far, "tile", [(i, ((i + 1) ^ 1) - 1) for i in range(1, peers - 1)])
    land = lax.all_to_all(
        msg.reshape(peers, 4, LANES), "tile", split_axis=0, concat_axis=0, tiled=True
    ).reshape(4 * peers, LANES)

    window = pltpu.VMEM((tiles, ROWS, LANES), F32)
    plane = pltpu.VMEM((OWN, width), F32)
    head, sub, sums = pl.pallas_call(
        route_kernel,
        out_shape=(array(OWN, width), array(OWN, width), array(peers, LANES)),
        in_specs=[vmem] * 8 + [outside] * 2,
        out_specs=(outside, outside, vmem),
        scratch_shapes=[pltpu.VMEM((384, LANES), F32)]
        + [window] * 11
        + [plane] * 3
        + [pltpu.VMEM((OWN, width), jnp.int32), pltpu.VMEM((4, OWN, width), F32)]
        + [pltpu.SemaphoreType.DMA((4,))],
        compiler_params=pltpu.CompilerParams(vmem_limit_bytes=16 * MIB),
        name="route",
    )(
        land, head_init, subsurface_init, conduct, drain_rate, flow_code, near, far,
        hbm(channel_share), hbm(cell_slot),
    )
    sums = lax.all_to_all(sums, "tile", split_axis=0, concat_axis=0, tiled=True)
    reach = pl.pallas_call(
        reach_kernel,
        out_shape=array(16, LANES),
        in_specs=[vmem] * 2,
        out_specs=vmem,
        compiler_params=pltpu.CompilerParams(vmem_limit_bytes=6 * MIB),
        name="reach_sums",
    )(land, sums)
    return (soil, head, sub, reach.reshape(-1))


def solution(mesh):
    rows = P(("member", "tile"), None)
    flat = P(("member", "tile"))
    return jax.shard_map(
        local,
        mesh=mesh,
        in_specs=(rows,) * 12 + (flat,),
        out_specs=(rows, rows, rows, flat),
        check_vma=False,
    )
```

```python
import jax
import jax.numpy as jnp
from jax import lax
from jax.experimental import pallas as pl
from jax.experimental.pallas import tpu as pltpu
from jax.sharding import PartitionSpec as P

ITERS = 6
HALO = 8
OWN = 32
ROWS = OWN + 2 * HALO
LANES = 128
F32 = jnp.float32
BF16 = jnp.bfloat16
MIB = 1024 * 1024


def iota(shape, dim):
    return lax.broadcasted_iota(jnp.int32, shape, dim)


def split3(x):
    a = x.astype(BF16).astype(F32)
    r = x - a
    b = r.astype(BF16).astype(F32)
    return a, b, r - b


def cut(j):
    return slice(LANES * j, LANES * (j + 1))


def left_of(tile, before):
    return jnp.where(iota(tile.shape, 1) == 0, before, tile)


def right_of(tile, after):
    return jnp.where(iota(tile.shape, 1) == LANES - 1, after, tile)


def water(p, s0, k, mask):
    wet = 2.0 * s0
    cap = k * (1.0 - wet)
    wet2 = wet * wet
    return mask * p * p / (p + cap), 0.25 * mask * k * (wet2 * wet2)


def send_kernel(
    precip, soil_init, ksat, land_mask, places, head, sub, conduct, drain, code,
    msg, near, far, turned, fields_in, mask_in, place_in, code_edge, sem,
):
    local = []
    for i, ref in enumerate((precip, soil_init, ksat)):
        local.append(pltpu.make_async_copy(ref, fields_in.at[i], sem.at[10 + i]))
    local.append(pltpu.make_async_copy(land_mask, mask_in, sem.at[14]))
    local.append(pltpu.make_async_copy(places, place_in, sem.at[15]))
    odd = lax.axis_index("tile") & 1
    near_rows = pl.ds(pl.multiple_of((1 - odd) * (OWN - HALO), HALO), HALO)
    far_rows = pl.ds(pl.multiple_of(odd * (OWN - HALO), HALO), HALO)
    copies = []
    for i, ref in enumerate((head, sub, conduct, drain)):
        into = slice(HALO * i, HALO * i + HALO)
        copies.append(pltpu.make_async_copy(ref.at[near_rows, :], near.at[into, :], sem.at[2 * i]))
        copies.append(pltpu.make_async_copy(ref.at[far_rows, :], far.at[into, :], sem.at[2 * i + 1]))
    codes = (
        pltpu.make_async_copy(code.at[near_rows, :], code_edge.at[0], sem.at[8]),
        pltpu.make_async_copy(code.at[far_rows, :], code_edge.at[1], sem.at[9]),
    )
    for c in local:
        c.start()
    for c in codes:
        c.start()
    for c in copies:
        c.start()
    for c in local:
        c.wait()
    p = fields_in[0]
    runoff, drainage = water(p, fields_in[1], fields_in[2], mask_in[...].astype(F32))
    rows = p.shape[1]
    fields = jnp.concatenate([runoff, drainage], axis=0)
    turned[0:8, :] = jnp.zeros((8, LANES), F32)
    turned[rows + 8 : rows + 16, :] = jnp.zeros((8, LANES), F32)
    turned[8 : rows + 8, :] = jnp.concatenate([fields] * 4, axis=0).T
    group = iota((32, LANES), 1) // 32
    for j in range(3):
        chunk = None
        for q in range(4):
            part = turned[pl.ds(6 + 4 * j + q, 32, stride=8), :]
            chunk = part if q == 0 else jnp.where(group == q, part, chunk)
        msg[pl.ds(j, 32, stride=4), :] = chunk
    place = place_in[...].astype(F32)
    msg[pl.ds(3, 16, stride=8), :] = place
    msg[pl.ds(7, 16, stride=8), :] = pltpu.roll(place, 64, 1)
    for c in codes:
        c.wait()
    near[4 * HALO :, :] = code_edge[0].astype(F32)
    far[4 * HALO :, :] = code_edge[1].astype(F32)
    for c in copies:
        c.wait()


def route_kernel(
    land, head_init, sub_init, conduct, drain, code, near, far, share, slot,
    precip, pet, soil_init, ksat, land_mask,
    head_out, sub_out, msg, soil_out,
    turned, h_a, h_b, s_a, s_b, g_w, a_w, dn_w, up_w, rt_w, lf_w, kp_w,
    head, sub, shares, slots, parts, fields_in, mask_in, soil, sem,
):
    tiles = g_w.shape[0]
    width = tiles * LANES
    zero = jnp.zeros((ROWS, LANES), F32)
    share_copy = pltpu.make_async_copy(share, shares, sem.at[0])
    slot_copy = pltpu.make_async_copy(slot, slots, sem.at[3])
    local = [pltpu.make_async_copy(land_mask, mask_in, sem.at[8])]
    for i, ref in enumerate((precip, pet, soil_init, ksat)):
        local.append(pltpu.make_async_copy(ref, fields_in.at[i], sem.at[4 + i]))
    share_copy.start()
    slot_copy.start()
    for c in local:
        c.start()

    odd = (lax.axis_index("tile") & 1) == 1

    def above(field, at):
        rows = slice(HALO * field, HALO * field + HALO)
        return jnp.where(odd, near[rows, at], far[rows, at])

    def below(field, at):
        rows = slice(HALO * field, HALO * field + HALO)
        return jnp.where(odd, far[rows, at], near[rows, at])

    def window(own, field, j):
        at = cut(j)
        return jnp.concatenate(
            [above(field, at), own[:, at].astype(F32), below(field, at)], axis=0
        )

    for j in range(tiles):
        g_w[j] = window(conduct, 2, j)
        d = window(drain, 3, j)
        k = window(code, 4, j)
        moves = [jnp.where(k == float(i), d, 0.0) for i in range(4)]
        dn_w[j], up_w[j], rt_w[j], lf_w[j] = moves
        kp_w[j] = 1.0 - (moves[0] + moves[1] + moves[2] + moves[3])
    for j in range(tiles):
        g = g_w[j]
        left = pltpu.roll(g_w[j - 1], 1, 1) if j > 0 else zero
        right = pltpu.roll(g_w[j + 1], LANES - 1, 1) if j < tiles - 1 else zero
        total = pltpu.roll(g, 1, 0) + pltpu.roll(g, ROWS - 1, 0)
        total = total + left_of(pltpu.roll(g, 1, 1), left)
        total = total + right_of(pltpu.roll(g, LANES - 1, 1), right)
        a_w[j] = 1.0 - g * total

    data = jnp.concatenate([land[pl.ds(j, 32, stride=4), :] for j in range(3)], axis=1)
    a, b, c = split3(data)
    turned[...] = jnp.concatenate([a, b, c, jnp.zeros_like(a)], axis=0).T
    lhs = jnp.concatenate([turned[pl.ds(q, 24, stride=16), :] for q in range(16)], axis=0)
    lhs = lhs.astype(BF16)
    low_half = iota((8, 256), 0) < 4
    src = iota((LANES, 256), 0)
    dst = iota((LANES, 256), 1)
    col = (iota((24, 256), 1) & 63) >> 2
    for n in range(width // 256):
        hot = ((src & 31) == ((dst + 256 * n) >> 6)) & (src < 96)
        spread = jnp.dot(lhs, jnp.where(hot, 1.0, 0.0).astype(BF16), preferred_element_type=F32)
        fine = spread[0:24]
        for q in range(1, 16):
            fine = jnp.where(col == q, spread[24 * q : 24 * q + 24], fine)
        for i in range(ROWS // 8):
            here = slice(8 * i, 8 * i + 8)
            at = slice(256 * n, 256 * n + 256)
            if i == 0:
                h0, s0 = above(0, at), above(1, at)
            elif i == ROWS // 8 - 1:
                h0, s0 = below(0, at), below(1, at)
            else:
                rows = slice(8 * i - 8, 8 * i)
                h0, s0 = head_init[rows, at], sub_init[rows, at]
            r = 4 * i
            h0 = h0 + jnp.where(low_half, fine[r : r + 1], fine[r + 2 : r + 3])
            s0 = s0 + jnp.where(low_half, fine[r + 1 : r + 2], fine[r + 3 : r + 4])
            for u in range(2):
                j = 2 * n + u
                h_a[j, here, :] = h0[:, cut(u)]
                s_a[j, here, :] = s0[:, cut(u)]

    def products(j, h_in, s_in):
        p = g_w[j] * h_in[j]
        s = s_in[j]
        return (
            p,
            pltpu.roll(p, 1, 1),
            pltpu.roll(p, LANES - 1, 1),
            pltpu.roll(rt_w[j] * s, 1, 1),
            pltpu.roll(lf_w[j] * s, LANES - 1, 1),
        )

    def substep(h_in, s_in, keep, take):
        before = (zero,) * 5
        now = products(0, h_in, s_in)
        for j in range(tiles):
            after = products(j + 1, h_in, s_in) if j < tiles - 1 else (zero,) * 5
            p = now[0]
            s = s_in[j]
            flux = pltpu.roll(p, 1, 0) + pltpu.roll(p, ROWS - 1, 0)
            flux = flux + left_of(now[1], before[1])
            flux = flux + right_of(now[2], after[2])
            new = pltpu.roll(dn_w[j] * s, 1, 0) + pltpu.roll(up_w[j] * s, ROWS - 1, 0)
            new = new + left_of(now[3], before[3])
            new = new + right_of(now[4], after[4])
            h = a_w[j, keep, :] * h_in[j, keep, :] + g_w[j, keep, :] * flux[keep]
            take(j, h, new[keep] + kp_w[j, keep, :] * s[keep])
            before, now = now, after

    def store(h_to, s_to):
        def take(j, h, s):
            h_to[j] = h
            s_to[j] = s

        return take

    def finish(j, h, s):
        at = cut(j)
        sub[:, at] = s
        inflow = shares[:, at] * h
        head[:, at] = h - inflow
        coarse = inflow.astype(BF16).astype(F32)
        parts[0, :, at] = coarse
        parts[1, :, at] = inflow - coarse
        q = slots[:, at]
        parts[2, :, at] = (q >> 6).astype(F32)
        parts[3, :, at] = (q & 63).astype(F32)

    source = (h_a, s_a)
    target = (h_b, s_b)
    for i in range(ITERS - 1):
        substep(*source, slice(0, ROWS), store(*target))
        source, target = target, source
    for c in local:
        c.wait()
    mask = mask_in[...].astype(F32)
    p, s0 = fields_in[0], fields_in[2]
    runoff, drainage = water(p, s0, fields_in[3], mask)
    evap = mask * fields_in[1] * (2.0 * s0)
    soil[...] = s0 + 0.1 * (mask * p - runoff - drainage - evap)
    soil_copy = pltpu.make_async_copy(soil, soil_out, sem.at[9])
    soil_copy.start()
    share_copy.wait()
    slot_copy.wait()
    substep(*source, slice(HALO, HALO + OWN), finish)
    head_copy = pltpu.make_async_copy(head, head_out, sem.at[1])
    sub_copy = pltpu.make_async_copy(sub, sub_out, sem.at[2])
    head_copy.start()
    sub_copy.start()

    owner = iota((32, width), 0).astype(F32).astype(BF16)
    place = iota((64, width), 0).astype(F32).astype(BF16)
    one = jnp.ones((64, width), BF16)
    none = jnp.zeros((64, width), BF16)

    def wide(i, r, n):
        return jnp.broadcast_to(parts[i, r : r + 1, :], (n, width)).astype(BF16)

    total = jnp.zeros((64, 64), F32)
    for r in range(OWN):
        hi = wide(2, r, 32) == owner
        lhs = jnp.concatenate([jnp.where(hi, wide(i, r, 32), none[0:32]) for i in range(2)], axis=0)
        rhs = jnp.where(wide(3, r, 64) == place, one, none)
        total = total + lax.dot_general(
            lhs, rhs, (((1,), (1,)), ((), ())), preferred_element_type=F32
        )
    total = total[0:32] + total[32:64]
    msg[...] = jnp.concatenate([total, jnp.zeros_like(total)], axis=1)
    soil_copy.wait()
    head_copy.wait()
    sub_copy.wait()


def reach_kernel(land, got, out):
    low = iota((16, LANES), 1) < 64

    def pack(x):
        return jnp.where(low, x[0:16], pltpu.roll(x[16:32], 64, 1))

    sums = pack(got[...])
    place = pack(land[pl.ds(3, 32, stride=4), :]).astype(jnp.int32)

    def line(x):
        return jnp.concatenate([x[u : u + 1] for u in range(16)], axis=1)

    width = 16 * LANES
    hi = line((place >> 7).astype(F32)) == iota((16, width), 0).astype(F32)
    lhs = jnp.concatenate([jnp.where(hi, line(x), 0.0) for x in split3(sums)], axis=0)
    lo = line((place & 127).astype(F32)) == iota((LANES, width), 0).astype(F32)
    total = lax.dot_general(
        lhs.astype(BF16), jnp.where(lo, 1.0, 0.0).astype(BF16),
        (((1,), (1,)), ((), ())), preferred_element_type=F32,
    )
    out[...] = total[0:16] + total[16:32] + total[32:48]


def local(
    precip,
    pet,
    soil_init,
    ksat,
    land_mask,
    head_init,
    subsurface_init,
    conduct,
    drain_rate,
    flow_code,
    channel_share,
    cell_slot,
    slot_reach,
):
    vmem = pl.BlockSpec(memory_space=pltpu.VMEM)
    outside = pl.BlockSpec(memory_space=pltpu.HBM)
    peers = lax.axis_size("tile")
    width = head_init.shape[1]
    tiles = width // LANES

    def hbm(x):
        return pltpu.with_memory_space_constraint(x, pltpu.HBM)

    def array(*shape):
        return jax.ShapeDtypeStruct(shape, F32)

    msg, near, far = pl.pallas_call(
        send_kernel,
        out_shape=(
            array(4 * peers, LANES), array(40, width), array(40, width),
        ),
        in_specs=[outside] * 10,
        out_specs=(vmem,) * 3,
        scratch_shapes=[
            pltpu.VMEM((precip.shape[1] + 16, LANES), F32),
            pltpu.VMEM((3,) + precip.shape, F32),
            pltpu.VMEM(precip.shape, jnp.int32),
            pltpu.VMEM((16, LANES), jnp.int32),
            pltpu.VMEM((2, 8, width), jnp.int32),
            pltpu.SemaphoreType.DMA((16,)),
        ],
        compiler_params=pltpu.CompilerParams(vmem_limit_bytes=6 * MIB),
        name="send",
    )(
        *map(
            hbm,
            (
                precip, soil_init, ksat, land_mask, slot_reach.reshape(-1, LANES),
                head_init, subsurface_init, conduct, drain_rate, flow_code,
            ),
        )
    )
    near = lax.ppermute(near, "tile", [(i, i ^ 1) for i in range(peers)])
    far = lax.ppermute(far, "tile", [(i, ((i + 1) ^ 1) - 1) for i in range(1, peers - 1)])
    land = lax.all_to_all(
        msg.reshape(peers, 4, LANES), "tile", split_axis=0, concat_axis=0, tiled=True
    ).reshape(4 * peers, LANES)

    window = pltpu.VMEM((tiles, ROWS, LANES), F32)
    plane = pltpu.VMEM((OWN, width), F32)
    head, sub, sums, soil = pl.pallas_call(
        route_kernel,
        out_shape=(
            array(OWN, width), array(OWN, width), array(peers, LANES), array(*precip.shape),
        ),
        in_specs=[vmem] * 8 + [outside] * 7,
        out_specs=(outside, outside, vmem, outside),
        scratch_shapes=[pltpu.VMEM((384, LANES), F32)]
        + [window] * 11
        + [plane] * 3
        + [pltpu.VMEM((OWN, width), jnp.int32), pltpu.VMEM((4, OWN, width), F32)]
        + [pltpu.VMEM((4,) + precip.shape, F32), pltpu.VMEM(precip.shape, jnp.int32)]
        + [pltpu.VMEM(precip.shape, F32), pltpu.SemaphoreType.DMA((10,))],
        compiler_params=pltpu.CompilerParams(vmem_limit_bytes=16 * MIB),
        name="route",
    )(
        land, head_init, subsurface_init, conduct, drain_rate, flow_code, near, far,
        *map(hbm, (channel_share, cell_slot, precip, pet, soil_init, ksat, land_mask)),
    )
    sums = lax.all_to_all(sums, "tile", split_axis=0, concat_axis=0, tiled=True)
    reach = pl.pallas_call(
        reach_kernel,
        out_shape=array(16, LANES),
        in_specs=[vmem] * 2,
        out_specs=vmem,
        compiler_params=pltpu.CompilerParams(vmem_limit_bytes=6 * MIB),
        name="reach_sums",
    )(land, sums)
    return (soil, head, sub, reach.reshape(-1))


def solution(mesh):
    rows = P(("member", "tile"), None)
    flat = P(("member", "tile"))
    return jax.shard_map(
        local,
        mesh=mesh,
        in_specs=(rows,) * 12 + (flat,),
        out_specs=(rows, rows, rows, flat),
        check_vma=False,
    )
```

```python
import jax
import jax.numpy as jnp
from jax import lax
from jax.experimental import pallas as pl
from jax.experimental.pallas import tpu as pltpu
from jax.sharding import PartitionSpec as P

ITERS = 6
HALO = 8
OWN = 32
ROWS = OWN + 2 * HALO
LANES = 128
F32 = jnp.float32
BF16 = jnp.bfloat16
MIB = 1024 * 1024


def iota(shape, dim):
    return lax.broadcasted_iota(jnp.int32, shape, dim)


def split3(x):
    a = x.astype(BF16).astype(F32)
    r = x - a
    b = r.astype(BF16).astype(F32)
    return a, b, r - b


def cut(j):
    return slice(LANES * j, LANES * (j + 1))


def left_of(tile, before):
    return jnp.where(iota(tile.shape, 1) == 0, before, tile)


def right_of(tile, after):
    return jnp.where(iota(tile.shape, 1) == LANES - 1, after, tile)


def water(p, s0, k, mask):
    wet = 2.0 * s0
    cap = k * (1.0 - wet)
    wet2 = wet * wet
    return mask * p * p / (p + cap), 0.25 * mask * k * (wet2 * wet2)


def send_kernel(
    precip, soil_init, ksat, land_mask, places, head, sub, conduct, drain, code,
    msg, near, far, turned, fields_in, mask_in, place_in, code_edge, sem,
):
    local = []
    for i, ref in enumerate((precip, soil_init, ksat)):
        local.append(pltpu.make_async_copy(ref, fields_in.at[i], sem.at[10 + i]))
    local.append(pltpu.make_async_copy(land_mask, mask_in, sem.at[14]))
    local.append(pltpu.make_async_copy(places, place_in, sem.at[15]))
    odd = lax.axis_index("tile") & 1
    near_rows = pl.ds(pl.multiple_of((1 - odd) * (OWN - HALO), HALO), HALO)
    far_rows = pl.ds(pl.multiple_of(odd * (OWN - HALO), HALO), HALO)
    copies = []
    for i, ref in enumerate((head, sub, conduct, drain)):
        into = slice(HALO * i, HALO * i + HALO)
        copies.append(pltpu.make_async_copy(ref.at[near_rows, :], near.at[into, :], sem.at[2 * i]))
        copies.append(pltpu.make_async_copy(ref.at[far_rows, :], far.at[into, :], sem.at[2 * i + 1]))
    codes = (
        pltpu.make_async_copy(code.at[near_rows, :], code_edge.at[0], sem.at[8]),
        pltpu.make_async_copy(code.at[far_rows, :], code_edge.at[1], sem.at[9]),
    )
    for c in local:
        c.start()
    for c in codes:
        c.start()
    for c in copies:
        c.start()
    for c in local:
        c.wait()
    p = fields_in[0]
    runoff, drainage = water(p, fields_in[1], fields_in[2], mask_in[...].astype(F32))
    rows = p.shape[1]
    fields = jnp.concatenate([runoff, drainage], axis=0)
    turned[0:8, :] = jnp.zeros((8, LANES), F32)
    turned[rows + 8 : rows + 16, :] = jnp.zeros((8, LANES), F32)
    turned[8 : rows + 8, :] = jnp.concatenate([fields] * 4, axis=0).T
    group = iota((32, LANES), 1) // 32
    for j in range(3):
        chunk = None
        for q in range(4):
            part = turned[pl.ds(6 + 4 * j + q, 32, stride=8), :]
            chunk = part if q == 0 else jnp.where(group == q, part, chunk)
        msg[pl.ds(j, 32, stride=4), :] = chunk
    place = place_in[...].astype(F32)
    msg[pl.ds(3, 16, stride=8), :] = place
    msg[pl.ds(7, 16, stride=8), :] = pltpu.roll(place, 64, 1)
    for c in codes:
        c.wait()
    near[4 * HALO :, :] = code_edge[0].astype(F32)
    far[4 * HALO :, :] = code_edge[1].astype(F32)
    for c in copies:
        c.wait()


def route_kernel(
    land, head_init, sub_init, conduct, drain, code, near, far, share, slot,
    precip, pet, soil_init, ksat, land_mask,
    head_out, sub_out, msg, soil_out,
    turned, h_a, h_b, s_a, s_b, g_w, a_w, dn_w, up_w, rt_w, lf_w, kp_w,
    head, sub, shares, slots, parts, fields_in, mask_in, soil, shifted, sem,
):
    tiles = g_w.shape[0]
    width = tiles * LANES
    zero = jnp.zeros((ROWS, LANES), F32)
    share_copy = pltpu.make_async_copy(share, shares, sem.at[0])
    slot_copy = pltpu.make_async_copy(slot, slots, sem.at[3])
    local = [pltpu.make_async_copy(land_mask, mask_in, sem.at[8])]
    for i, ref in enumerate((precip, pet, soil_init, ksat)):
        local.append(pltpu.make_async_copy(ref, fields_in.at[i], sem.at[4 + i]))
    share_copy.start()
    slot_copy.start()
    for c in local:
        c.start()

    odd = (lax.axis_index("tile") & 1) == 1

    def above(field, at):
        rows = slice(HALO * field, HALO * field + HALO)
        return jnp.where(odd, near[rows, at], far[rows, at])

    def below(field, at):
        rows = slice(HALO * field, HALO * field + HALO)
        return jnp.where(odd, far[rows, at], near[rows, at])

    def window(own, field, j):
        at = cut(j)
        return jnp.concatenate(
            [above(field, at), own[:, at].astype(F32), below(field, at)], axis=0
        )

    for j in range(tiles):
        g_w[j] = window(conduct, 2, j)
        d = window(drain, 3, j)
        k = window(code, 4, j)
        moves = [jnp.where(k == float(i), d, 0.0) for i in range(4)]
        dn_w[j], up_w[j], rt_w[j], lf_w[j] = moves
        kp_w[j] = 1.0 - (moves[0] + moves[1] + moves[2] + moves[3])
    for j in range(tiles):
        g = g_w[j]
        left = pltpu.roll(g_w[j - 1], 1, 1) if j > 0 else zero
        right = pltpu.roll(g_w[j + 1], LANES - 1, 1) if j < tiles - 1 else zero
        total = pltpu.roll(g, 1, 0) + pltpu.roll(g, ROWS - 1, 0)
        total = total + left_of(pltpu.roll(g, 1, 1), left)
        total = total + right_of(pltpu.roll(g, LANES - 1, 1), right)
        a_w[j] = 1.0 - g * total

    data = jnp.concatenate([land[pl.ds(j, 32, stride=4), :] for j in range(3)], axis=1)
    a, b, c = split3(data)
    turned[...] = jnp.concatenate([a, b, c, jnp.zeros_like(a)], axis=0).T
    lhs = jnp.concatenate([turned[pl.ds(q, 24, stride=16), :] for q in range(16)], axis=0)
    lhs = lhs.astype(BF16)
    low_half = iota((8, 256), 0) < 4
    src = iota((LANES, 256), 0)
    dst = iota((LANES, 256), 1)
    col = (iota((24, 256), 1) & 63) >> 2
    for n in range(width // 256):
        hot = ((src & 31) == ((dst + 256 * n) >> 6)) & (src < 96)
        spread = jnp.dot(lhs, jnp.where(hot, 1.0, 0.0).astype(BF16), preferred_element_type=F32)
        fine = spread[0:24]
        for q in range(1, 16):
            fine = jnp.where(col == q, spread[24 * q : 24 * q + 24], fine)
        for i in range(ROWS // 8):
            here = slice(8 * i, 8 * i + 8)
            at = slice(256 * n, 256 * n + 256)
            if i == 0:
                h0, s0 = above(0, at), above(1, at)
            elif i == ROWS // 8 - 1:
                h0, s0 = below(0, at), below(1, at)
            else:
                rows = slice(8 * i - 8, 8 * i)
                h0, s0 = head_init[rows, at], sub_init[rows, at]
            r = 4 * i
            h0 = h0 + jnp.where(low_half, fine[r : r + 1], fine[r + 2 : r + 3])
            s0 = s0 + jnp.where(low_half, fine[r + 1 : r + 2], fine[r + 3 : r + 4])
            for u in range(2):
                j = 2 * n + u
                h_a[j, here, :] = h0[:, cut(u)]
                s_a[j, here, :] = s0[:, cut(u)]

    edge = jnp.zeros((3, tiles, 8, LANES), F32)
    shifted[:, :, 0:8, :] = edge
    shifted[:, :, ROWS + 8 : ROWS + 16, :] = edge

    def products(j, h_in, s_in):
        p = g_w[j] * h_in[j]
        s = s_in[j]
        return (
            p,
            pltpu.roll(p, 1, 1),
            pltpu.roll(p, LANES - 1, 1),
            pltpu.roll(rt_w[j] * s, 1, 1),
            pltpu.roll(lf_w[j] * s, LANES - 1, 1),
        )

    def substep(h_in, s_in, keep, take):
        before = (zero,) * 5
        now = products(0, h_in, s_in)
        for j in range(tiles):
            after = products(j + 1, h_in, s_in) if j < tiles - 1 else (zero,) * 5
            p = now[0]
            s = s_in[j]
            shifted[0, j, 8 : ROWS + 8, :] = p
            above_at = slice(keep.start + 7, keep.stop + 7)
            below_at = slice(keep.start + 9, keep.stop + 9)
            flux = shifted[0, j, above_at, :] + shifted[0, j, below_at, :]
            flux = flux + left_of(now[1], before[1])[keep]
            flux = flux + right_of(now[2], after[2])[keep]
            shifted[1, j, 8 : ROWS + 8, :] = dn_w[j] * s
            shifted[2, j, 8 : ROWS + 8, :] = up_w[j] * s
            new = shifted[1, j, above_at, :] + shifted[2, j, below_at, :]
            new = new + left_of(now[3], before[3])[keep]
            new = new + right_of(now[4], after[4])[keep]
            h = a_w[j, keep, :] * h_in[j, keep, :] + g_w[j, keep, :] * flux
            take(j, h, new + kp_w[j, keep, :] * s[keep])
            before, now = now, after

    def store(h_to, s_to):
        def take(j, h, s):
            h_to[j] = h
            s_to[j] = s

        return take

    def finish(j, h, s):
        at = cut(j)
        sub[:, at] = s
        inflow = shares[:, at] * h
        head[:, at] = h - inflow
        coarse = inflow.astype(BF16).astype(F32)
        parts[0, :, at] = coarse
        parts[1, :, at] = inflow - coarse
        q = slots[:, at]
        parts[2, :, at] = (q >> 6).astype(F32)
        parts[3, :, at] = (q & 63).astype(F32)

    source = (h_a, s_a)
    target = (h_b, s_b)
    for i in range(ITERS - 1):
        substep(*source, slice(0, ROWS), store(*target))
        source, target = target, source
    for c in local:
        c.wait()
    mask = mask_in[...].astype(F32)
    p, s0 = fields_in[0], fields_in[2]
    runoff, drainage = water(p, s0, fields_in[3], mask)
    evap = mask * fields_in[1] * (2.0 * s0)
    soil[...] = s0 + 0.1 * (mask * p - runoff - drainage - evap)
    soil_copy = pltpu.make_async_copy(soil, soil_out, sem.at[9])
    soil_copy.start()
    share_copy.wait()
    slot_copy.wait()
    substep(*source, slice(HALO, HALO + OWN), finish)
    head_copy = pltpu.make_async_copy(head, head_out, sem.at[1])
    sub_copy = pltpu.make_async_copy(sub, sub_out, sem.at[2])
    head_copy.start()
    sub_copy.start()

    owner = iota((32, width), 0).astype(F32).astype(BF16)
    place = iota((64, width), 0).astype(F32).astype(BF16)
    one = jnp.ones((64, width), BF16)
    none = jnp.zeros((64, width), BF16)

    def wide(i, r, n):
        return jnp.broadcast_to(parts[i, r : r + 1, :], (n, width)).astype(BF16)

    total = jnp.zeros((64, 64), F32)
    for r in range(OWN):
        hi = wide(2, r, 32) == owner
        lhs = jnp.concatenate([jnp.where(hi, wide(i, r, 32), none[0:32]) for i in range(2)], axis=0)
        rhs = jnp.where(wide(3, r, 64) == place, one, none)
        total = total + lax.dot_general(
            lhs, rhs, (((1,), (1,)), ((), ())), preferred_element_type=F32
        )
    total = total[0:32] + total[32:64]
    msg[...] = jnp.concatenate([total, jnp.zeros_like(total)], axis=1)
    soil_copy.wait()
    head_copy.wait()
    sub_copy.wait()


def reach_kernel(land, got, out):
    low = iota((16, LANES), 1) < 64

    def pack(x):
        return jnp.where(low, x[0:16], pltpu.roll(x[16:32], 64, 1))

    sums = pack(got[...])
    place = pack(land[pl.ds(3, 32, stride=4), :]).astype(jnp.int32)

    def line(x):
        return jnp.concatenate([x[u : u + 1] for u in range(16)], axis=1)

    width = 16 * LANES
    hi = line((place >> 7).astype(F32)) == iota((16, width), 0).astype(F32)
    lhs = jnp.concatenate([jnp.where(hi, line(x), 0.0) for x in split3(sums)], axis=0)
    lo = line((place & 127).astype(F32)) == iota((LANES, width), 0).astype(F32)
    total = lax.dot_general(
        lhs.astype(BF16), jnp.where(lo, 1.0, 0.0).astype(BF16),
        (((1,), (1,)), ((), ())), preferred_element_type=F32,
    )
    out[...] = total[0:16] + total[16:32] + total[32:48]


def local(
    precip,
    pet,
    soil_init,
    ksat,
    land_mask,
    head_init,
    subsurface_init,
    conduct,
    drain_rate,
    flow_code,
    channel_share,
    cell_slot,
    slot_reach,
):
    vmem = pl.BlockSpec(memory_space=pltpu.VMEM)
    outside = pl.BlockSpec(memory_space=pltpu.HBM)
    peers = lax.axis_size("tile")
    width = head_init.shape[1]
    tiles = width // LANES

    def hbm(x):
        return pltpu.with_memory_space_constraint(x, pltpu.HBM)

    def array(*shape):
        return jax.ShapeDtypeStruct(shape, F32)

    msg, near, far = pl.pallas_call(
        send_kernel,
        out_shape=(
            array(4 * peers, LANES), array(40, width), array(40, width),
        ),
        in_specs=[outside] * 10,
        out_specs=(vmem,) * 3,
        scratch_shapes=[
            pltpu.VMEM((precip.shape[1] + 16, LANES), F32),
            pltpu.VMEM((3,) + precip.shape, F32),
            pltpu.VMEM(precip.shape, jnp.int32),
            pltpu.VMEM((16, LANES), jnp.int32),
            pltpu.VMEM((2, 8, width), jnp.int32),
            pltpu.SemaphoreType.DMA((16,)),
        ],
        compiler_params=pltpu.CompilerParams(vmem_limit_bytes=6 * MIB),
        name="send",
    )(
        *map(
            hbm,
            (
                precip, soil_init, ksat, land_mask, slot_reach.reshape(-1, LANES),
                head_init, subsurface_init, conduct, drain_rate, flow_code,
            ),
        )
    )
    near = lax.ppermute(near, "tile", [(i, i ^ 1) for i in range(peers)])
    far = lax.ppermute(far, "tile", [(i, ((i + 1) ^ 1) - 1) for i in range(1, peers - 1)])
    land = lax.all_to_all(
        msg.reshape(peers, 4, LANES), "tile", split_axis=0, concat_axis=0, tiled=True
    ).reshape(4 * peers, LANES)

    window = pltpu.VMEM((tiles, ROWS, LANES), F32)
    plane = pltpu.VMEM((OWN, width), F32)
    head, sub, sums, soil = pl.pallas_call(
        route_kernel,
        out_shape=(
            array(OWN, width), array(OWN, width), array(peers, LANES), array(*precip.shape),
        ),
        in_specs=[vmem] * 8 + [outside] * 7,
        out_specs=(outside, outside, vmem, outside),
        scratch_shapes=[pltpu.VMEM((384, LANES), F32)]
        + [window] * 11
        + [plane] * 3
        + [pltpu.VMEM((OWN, width), jnp.int32), pltpu.VMEM((4, OWN, width), F32)]
        + [pltpu.VMEM((4,) + precip.shape, F32), pltpu.VMEM(precip.shape, jnp.int32)]
        + [pltpu.VMEM(precip.shape, F32), pltpu.VMEM((3, tiles, ROWS + 16, LANES), F32)]
        + [pltpu.SemaphoreType.DMA((10,))],
        compiler_params=pltpu.CompilerParams(vmem_limit_bytes=16 * MIB),
        name="route",
    )(
        land, head_init, subsurface_init, conduct, drain_rate, flow_code, near, far,
        *map(hbm, (channel_share, cell_slot, precip, pet, soil_init, ksat, land_mask)),
    )
    sums = lax.all_to_all(sums, "tile", split_axis=0, concat_axis=0, tiled=True)
    reach = pl.pallas_call(
        reach_kernel,
        out_shape=array(16, LANES),
        in_specs=[vmem] * 2,
        out_specs=vmem,
        compiler_params=pltpu.CompilerParams(vmem_limit_bytes=6 * MIB),
        name="reach_sums",
    )(land, sums)
    return (soil, head, sub, reach.reshape(-1))


def solution(mesh):
    rows = P(("member", "tile"), None)
    flat = P(("member", "tile"))
    return jax.shard_map(
        local,
        mesh=mesh,
        in_specs=(rows,) * 12 + (flat,),
        out_specs=(rows, rows, rows, flat),
        check_vma=False,
    )
```

```python
import jax
import jax.numpy as jnp
from jax import lax
from jax.experimental import pallas as pl
from jax.experimental.pallas import tpu as pltpu
from jax.sharding import PartitionSpec as P

ITERS = 6
HALO = 8
OWN = 32
ROWS = OWN + 2 * HALO
LANES = 128
F32 = jnp.float32
BF16 = jnp.bfloat16
MIB = 1024 * 1024


def iota(shape, dim):
    return lax.broadcasted_iota(jnp.int32, shape, dim)


def split3(x):
    a = x.astype(BF16).astype(F32)
    r = x - a
    b = r.astype(BF16).astype(F32)
    return a, b, r - b


def cut(j):
    return slice(LANES * j, LANES * (j + 1))


def left_of(tile, before):
    return jnp.where(iota(tile.shape, 1) == 0, before, tile)


def right_of(tile, after):
    return jnp.where(iota(tile.shape, 1) == LANES - 1, after, tile)


def water(p, s0, k, mask):
    wet = 2.0 * s0
    cap = k * (1.0 - wet)
    wet2 = wet * wet
    return mask * p * p / (p + cap), 0.25 * mask * k * (wet2 * wet2)


def send_kernel(
    precip, soil_init, ksat, land_mask, places, head, sub, conduct, drain, code,
    msg, near, far, turned, fields_in, mask_in, place_in, code_edge, sem,
):
    local = []
    for i, ref in enumerate((precip, soil_init, ksat)):
        local.append(pltpu.make_async_copy(ref, fields_in.at[i], sem.at[10 + i]))
    local.append(pltpu.make_async_copy(land_mask, mask_in, sem.at[14]))
    local.append(pltpu.make_async_copy(places, place_in, sem.at[15]))
    odd = lax.axis_index("tile") & 1
    near_rows = pl.ds(pl.multiple_of((1 - odd) * (OWN - HALO), HALO), HALO)
    far_rows = pl.ds(pl.multiple_of(odd * (OWN - HALO), HALO), HALO)
    copies = []
    for i, ref in enumerate((head, sub, conduct, drain)):
        into = slice(HALO * i, HALO * i + HALO)
        copies.append(pltpu.make_async_copy(ref.at[near_rows, :], near.at[into, :], sem.at[2 * i]))
        copies.append(pltpu.make_async_copy(ref.at[far_rows, :], far.at[into, :], sem.at[2 * i + 1]))
    codes = (
        pltpu.make_async_copy(code.at[near_rows, :], code_edge.at[0], sem.at[8]),
        pltpu.make_async_copy(code.at[far_rows, :], code_edge.at[1], sem.at[9]),
    )
    for c in local:
        c.start()
    for c in codes:
        c.start()
    for c in copies:
        c.start()
    for c in local:
        c.wait()
    p = fields_in[0]
    runoff, drainage = water(p, fields_in[1], fields_in[2], mask_in[...].astype(F32))
    rows = p.shape[1]
    fields = jnp.concatenate([runoff, drainage], axis=0)
    turned[0:8, :] = jnp.zeros((8, LANES), F32)
    turned[rows + 8 : rows + 16, :] = jnp.zeros((8, LANES), F32)
    turned[8 : rows + 8, :] = jnp.concatenate([fields] * 4, axis=0).T
    group = iota((32, LANES), 1) // 32
    for j in range(3):
        chunk = None
        for q in range(4):
            part = turned[pl.ds(6 + 4 * j + q, 32, stride=8), :]
            chunk = part if q == 0 else jnp.where(group == q, part, chunk)
        msg[pl.ds(j, 32, stride=4), :] = chunk
    place = place_in[...].astype(F32)
    msg[pl.ds(3, 16, stride=8), :] = place
    msg[pl.ds(7, 16, stride=8), :] = pltpu.roll(place, 64, 1)
    for c in codes:
        c.wait()
    near[4 * HALO :, :] = code_edge[0].astype(F32)
    far[4 * HALO :, :] = code_edge[1].astype(F32)
    for c in copies:
        c.wait()


def route_kernel(
    land, head_init, sub_init, conduct, drain, code, near, far, share, slot,
    precip, pet, soil_init, ksat, land_mask,
    head_out, sub_out, msg, soil_out,
    turned, h_a, h_b, s_a, s_b, g_w, a_w, dn_w, up_w, rt_w, lf_w, kp_w,
    head, sub, shares, slots, parts, fields_in, mask_in, soil, shifted, sem,
):
    tiles = g_w.shape[0]
    width = tiles * LANES
    zero = jnp.zeros((ROWS, LANES), F32)
    share_copy = pltpu.make_async_copy(share, shares, sem.at[0])
    slot_copy = pltpu.make_async_copy(slot, slots, sem.at[3])
    local = [pltpu.make_async_copy(land_mask, mask_in, sem.at[8])]
    for i, ref in enumerate((precip, pet, soil_init, ksat)):
        local.append(pltpu.make_async_copy(ref, fields_in.at[i], sem.at[4 + i]))
    share_copy.start()
    slot_copy.start()
    for c in local:
        c.start()

    odd = (lax.axis_index("tile") & 1) == 1

    def above(field, at):
        rows = slice(HALO * field, HALO * field + HALO)
        return jnp.where(odd, near[rows, at], far[rows, at])

    def below(field, at):
        rows = slice(HALO * field, HALO * field + HALO)
        return jnp.where(odd, far[rows, at], near[rows, at])

    def window(own, field, j):
        at = cut(j)
        return jnp.concatenate(
            [above(field, at), own[:, at].astype(F32), below(field, at)], axis=0
        )

    for j in range(tiles):
        g_w[j] = window(conduct, 2, j)
        d = window(drain, 3, j)
        k = window(code, 4, j)
        moves = [jnp.where(k == float(i), d, 0.0) for i in range(4)]
        dn_w[j], up_w[j], rt_w[j], lf_w[j] = moves
        kp_w[j] = 1.0 - (moves[0] + moves[1] + moves[2] + moves[3])
    for j in range(tiles):
        g = g_w[j]
        left = pltpu.roll(g_w[j - 1], 1, 1) if j > 0 else zero
        right = pltpu.roll(g_w[j + 1], LANES - 1, 1) if j < tiles - 1 else zero
        total = pltpu.roll(g, 1, 0) + pltpu.roll(g, ROWS - 1, 0)
        total = total + left_of(pltpu.roll(g, 1, 1), left)
        total = total + right_of(pltpu.roll(g, LANES - 1, 1), right)
        a_w[j] = 1.0 - g * total

    data = jnp.concatenate([land[pl.ds(j, 32, stride=4), :] for j in range(3)], axis=1)
    a, b, c = split3(data)
    turned[...] = jnp.concatenate([a, b, c, jnp.zeros_like(a)], axis=0).T
    lhs = jnp.concatenate([turned[pl.ds(q, 24, stride=16), :] for q in range(16)], axis=0)
    lhs = lhs.astype(BF16)
    low_half = iota((8, 256), 0) < 4
    src = iota((LANES, 256), 0)
    dst = iota((LANES, 256), 1)
    col = (iota((24, 256), 1) & 63) >> 2
    for n in range(width // 256):
        hot = ((src & 31) == ((dst + 256 * n) >> 6)) & (src < 96)
        spread = jnp.dot(lhs, jnp.where(hot, 1.0, 0.0).astype(BF16), preferred_element_type=F32)
        fine = spread[0:24]
        for q in range(1, 16):
            fine = jnp.where(col == q, spread[24 * q : 24 * q + 24], fine)
        for i in range(ROWS // 8):
            here = slice(8 * i, 8 * i + 8)
            at = slice(256 * n, 256 * n + 256)
            if i == 0:
                h0, s0 = above(0, at), above(1, at)
            elif i == ROWS // 8 - 1:
                h0, s0 = below(0, at), below(1, at)
            else:
                rows = slice(8 * i - 8, 8 * i)
                h0, s0 = head_init[rows, at], sub_init[rows, at]
            r = 4 * i
            h0 = h0 + jnp.where(low_half, fine[r : r + 1], fine[r + 2 : r + 3])
            s0 = s0 + jnp.where(low_half, fine[r + 1 : r + 2], fine[r + 3 : r + 4])
            for u in range(2):
                j = 2 * n + u
                h_a[j, here, :] = h0[:, cut(u)]
                s_a[j, here, :] = s0[:, cut(u)]

    edge = jnp.zeros((3, tiles, 8, LANES), F32)
    shifted[:, :, 0:8, :] = edge
    shifted[:, :, ROWS + 8 : ROWS + 16, :] = edge

    def around(keep):
        up_rows = slice(keep.start + 7, keep.stop + 7)
        down_rows = slice(keep.start + 9, keep.stop + 9)
        return up_rows, down_rows

    def head_step(h_in, keep, take):
        above_at, below_at = around(keep)

        def products(j):
            p = g_w[j] * h_in[j]
            return p, pltpu.roll(p, 1, 1), pltpu.roll(p, LANES - 1, 1)

        before = zero
        now = products(0)
        for j in range(tiles):
            after = products(j + 1) if j < tiles - 1 else (zero,) * 3
            shifted[0, j, 8 : ROWS + 8, :] = now[0]
            flux = shifted[0, j, above_at, :] + shifted[0, j, below_at, :]
            flux = flux + left_of(now[1], before)[keep]
            flux = flux + right_of(now[2], after[2])[keep]
            take(j, a_w[j, keep, :] * h_in[j, keep, :] + g_w[j, keep, :] * flux)
            before, now = now[1], after

    def sub_step(s_in, keep, take):
        above_at, below_at = around(keep)

        def products(j):
            s = s_in[j]
            return pltpu.roll(rt_w[j] * s, 1, 1), pltpu.roll(lf_w[j] * s, LANES - 1, 1)

        before = zero
        now = products(0)
        for j in range(tiles):
            after = products(j + 1) if j < tiles - 1 else (zero,) * 2
            s = s_in[j]
            shifted[1, j, 8 : ROWS + 8, :] = dn_w[j] * s
            shifted[2, j, 8 : ROWS + 8, :] = up_w[j] * s
            new = shifted[1, j, above_at, :] + shifted[2, j, below_at, :]
            new = new + left_of(now[0], before)[keep]
            new = new + right_of(now[1], after[1])[keep]
            take(j, new + kp_w[j, keep, :] * s[keep])
            before, now = now[0], after

    def store(to):
        def take(j, x):
            to[j] = x

        return take

    def finish_sub(j, s):
        sub[:, cut(j)] = s

    def finish(j, h):
        at = cut(j)
        inflow = shares[:, at] * h
        head[:, at] = h - inflow
        coarse = inflow.astype(BF16).astype(F32)
        parts[0, :, at] = coarse
        parts[1, :, at] = inflow - coarse

    source = (h_a, s_a)
    target = (h_b, s_b)
    for i in range(ITERS - 1):
        sub_step(source[1], slice(0, ROWS), store(target[1]))
        source, target = target, source
    sub_step(source[1], slice(HALO, HALO + OWN), finish_sub)
    sub_copy = pltpu.make_async_copy(sub, sub_out, sem.at[2])
    sub_copy.start()
    for c in local:
        c.wait()
    mask = mask_in[...].astype(F32)
    p, s0 = fields_in[0], fields_in[2]
    runoff, drainage = water(p, s0, fields_in[3], mask)
    evap = mask * fields_in[1] * (2.0 * s0)
    soil[...] = s0 + 0.1 * (mask * p - runoff - drainage - evap)
    soil_copy = pltpu.make_async_copy(soil, soil_out, sem.at[9])
    soil_copy.start()
    share_copy.wait()
    slot_copy.wait()
    parts[2] = (slots[...] >> 6).astype(F32)
    parts[3] = (slots[...] & 63).astype(F32)
    source, target = (h_a, s_a), (h_b, s_b)
    for i in range(ITERS - 1):
        head_step(source[0], slice(0, ROWS), store(target[0]))
        source, target = target, source
    head_step(source[0], slice(HALO, HALO + OWN), finish)
    head_copy = pltpu.make_async_copy(head, head_out, sem.at[1])
    head_copy.start()

    owner = iota((32, width), 0).astype(F32).astype(BF16)
    place = iota((64, width), 0).astype(F32).astype(BF16)
    one = jnp.ones((64, width), BF16)
    none = jnp.zeros((64, width), BF16)

    def wide(i, r, n):
        return jnp.broadcast_to(parts[i, r : r + 1, :], (n, width)).astype(BF16)

    total = jnp.zeros((64, 64), F32)
    for r in range(OWN):
        hi = wide(2, r, 32) == owner
        lhs = jnp.concatenate([jnp.where(hi, wide(i, r, 32), none[0:32]) for i in range(2)], axis=0)
        rhs = jnp.where(wide(3, r, 64) == place, one, none)
        total = total + lax.dot_general(
            lhs, rhs, (((1,), (1,)), ((), ())), preferred_element_type=F32
        )
    total = total[0:32] + total[32:64]
    msg[...] = jnp.concatenate([total, jnp.zeros_like(total)], axis=1)
    soil_copy.wait()
    head_copy.wait()
    sub_copy.wait()


def reach_kernel(land, got, out):
    low = iota((16, LANES), 1) < 64

    def pack(x):
        return jnp.where(low, x[0:16], pltpu.roll(x[16:32], 64, 1))

    sums = pack(got[...])
    place = pack(land[pl.ds(3, 32, stride=4), :]).astype(jnp.int32)

    def line(x):
        return jnp.concatenate([x[u : u + 1] for u in range(16)], axis=1)

    width = 16 * LANES
    hi = line((place >> 7).astype(F32)) == iota((16, width), 0).astype(F32)
    lhs = jnp.concatenate([jnp.where(hi, line(x), 0.0) for x in split3(sums)], axis=0)
    lo = line((place & 127).astype(F32)) == iota((LANES, width), 0).astype(F32)
    total = lax.dot_general(
        lhs.astype(BF16), jnp.where(lo, 1.0, 0.0).astype(BF16),
        (((1,), (1,)), ((), ())), preferred_element_type=F32,
    )
    out[...] = total[0:16] + total[16:32] + total[32:48]


def local(
    precip,
    pet,
    soil_init,
    ksat,
    land_mask,
    head_init,
    subsurface_init,
    conduct,
    drain_rate,
    flow_code,
    channel_share,
    cell_slot,
    slot_reach,
):
    vmem = pl.BlockSpec(memory_space=pltpu.VMEM)
    outside = pl.BlockSpec(memory_space=pltpu.HBM)
    peers = lax.axis_size("tile")
    width = head_init.shape[1]
    tiles = width // LANES

    def hbm(x):
        return pltpu.with_memory_space_constraint(x, pltpu.HBM)

    def array(*shape):
        return jax.ShapeDtypeStruct(shape, F32)

    msg, near, far = pl.pallas_call(
        send_kernel,
        out_shape=(
            array(4 * peers, LANES), array(40, width), array(40, width),
        ),
        in_specs=[outside] * 10,
        out_specs=(vmem,) * 3,
        scratch_shapes=[
            pltpu.VMEM((precip.shape[1] + 16, LANES), F32),
            pltpu.VMEM((3,) + precip.shape, F32),
            pltpu.VMEM(precip.shape, jnp.int32),
            pltpu.VMEM((16, LANES), jnp.int32),
            pltpu.VMEM((2, 8, width), jnp.int32),
            pltpu.SemaphoreType.DMA((16,)),
        ],
        compiler_params=pltpu.CompilerParams(vmem_limit_bytes=6 * MIB),
        name="send",
    )(
        *map(
            hbm,
            (
                precip, soil_init, ksat, land_mask, slot_reach.reshape(-1, LANES),
                head_init, subsurface_init, conduct, drain_rate, flow_code,
            ),
        )
    )
    near = lax.ppermute(near, "tile", [(i, i ^ 1) for i in range(peers)])
    far = lax.ppermute(far, "tile", [(i, ((i + 1) ^ 1) - 1) for i in range(1, peers - 1)])
    land = lax.all_to_all(
        msg.reshape(peers, 4, LANES), "tile", split_axis=0, concat_axis=0, tiled=True
    ).reshape(4 * peers, LANES)

    window = pltpu.VMEM((tiles, ROWS, LANES), F32)
    plane = pltpu.VMEM((OWN, width), F32)
    head, sub, sums, soil = pl.pallas_call(
        route_kernel,
        out_shape=(
            array(OWN, width), array(OWN, width), array(peers, LANES), array(*precip.shape),
        ),
        in_specs=[vmem] * 8 + [outside] * 7,
        out_specs=(outside, outside, vmem, outside),
        scratch_shapes=[pltpu.VMEM((384, LANES), F32)]
        + [window] * 11
        + [plane] * 3
        + [pltpu.VMEM((OWN, width), jnp.int32), pltpu.VMEM((4, OWN, width), F32)]
        + [pltpu.VMEM((4,) + precip.shape, F32), pltpu.VMEM(precip.shape, jnp.int32)]
        + [pltpu.VMEM(precip.shape, F32), pltpu.VMEM((3, tiles, ROWS + 16, LANES), F32)]
        + [pltpu.SemaphoreType.DMA((10,))],
        compiler_params=pltpu.CompilerParams(vmem_limit_bytes=16 * MIB),
        name="route",
    )(
        land, head_init, subsurface_init, conduct, drain_rate, flow_code, near, far,
        *map(hbm, (channel_share, cell_slot, precip, pet, soil_init, ksat, land_mask)),
    )
    sums = lax.all_to_all(sums, "tile", split_axis=0, concat_axis=0, tiled=True)
    reach = pl.pallas_call(
        reach_kernel,
        out_shape=array(16, LANES),
        in_specs=[vmem] * 2,
        out_specs=vmem,
        compiler_params=pltpu.CompilerParams(vmem_limit_bytes=6 * MIB),
        name="reach_sums",
    )(land, sums)
    return (soil, head, sub, reach.reshape(-1))


def solution(mesh):
    rows = P(("member", "tile"), None)
    flat = P(("member", "tile"))
    return jax.shard_map(
        local,
        mesh=mesh,
        in_specs=(rows,) * 12 + (flat,),
        out_specs=(rows, rows, rows, flat),
        check_vma=False,
    )
```

```python
import jax
import jax.numpy as jnp
from jax import lax
from jax.experimental import pallas as pl
from jax.experimental.pallas import tpu as pltpu
from jax.sharding import PartitionSpec as P

ITERS = 6
HALO = 8
OWN = 32
ROWS = OWN + 2 * HALO
LANES = 128
F32 = jnp.float32
BF16 = jnp.bfloat16
MIB = 1024 * 1024


def iota(shape, dim):
    return lax.broadcasted_iota(jnp.int32, shape, dim)


def split3(x):
    a = x.astype(BF16).astype(F32)
    r = x - a
    b = r.astype(BF16).astype(F32)
    return a, b, r - b


def cut(j):
    return slice(LANES * j, LANES * (j + 1))


def left_of(tile, before):
    return jnp.where(iota(tile.shape, 1) == 0, before, tile)


def right_of(tile, after):
    return jnp.where(iota(tile.shape, 1) == LANES - 1, after, tile)


def water(p, s0, k, mask):
    wet = 2.0 * s0
    cap = k * (1.0 - wet)
    wet2 = wet * wet
    return mask * p * p / (p + cap), 0.25 * mask * k * (wet2 * wet2)


def send_kernel(
    precip, soil_init, ksat, land_mask, places, head, sub, conduct, drain, code,
    msg, near, far, turned, fields_in, mask_in, place_in, code_edge, sem,
):
    local = []
    for i, ref in enumerate((precip, soil_init, ksat)):
        local.append(pltpu.make_async_copy(ref, fields_in.at[i], sem.at[10 + i]))
    local.append(pltpu.make_async_copy(land_mask, mask_in, sem.at[14]))
    local.append(pltpu.make_async_copy(places, place_in, sem.at[15]))
    odd = lax.axis_index("tile") & 1
    near_rows = pl.ds(pl.multiple_of((1 - odd) * (OWN - HALO), HALO), HALO)
    far_rows = pl.ds(pl.multiple_of(odd * (OWN - HALO), HALO), HALO)
    copies = []
    for i, ref in enumerate((head, sub, conduct, drain)):
        into = slice(HALO * i, HALO * i + HALO)
        copies.append(pltpu.make_async_copy(ref.at[near_rows, :], near.at[into, :], sem.at[2 * i]))
        copies.append(pltpu.make_async_copy(ref.at[far_rows, :], far.at[into, :], sem.at[2 * i + 1]))
    codes = (
        pltpu.make_async_copy(code.at[near_rows, :], code_edge.at[0], sem.at[8]),
        pltpu.make_async_copy(code.at[far_rows, :], code_edge.at[1], sem.at[9]),
    )
    for c in local:
        c.start()
    for c in codes:
        c.start()
    for c in copies:
        c.start()
    for c in local:
        c.wait()
    p = fields_in[0]
    runoff, drainage = water(p, fields_in[1], fields_in[2], mask_in[...].astype(F32))
    rows = p.shape[1]
    fields = jnp.concatenate([runoff, drainage], axis=0)
    turned[0:8, :] = jnp.zeros((8, LANES), F32)
    turned[rows + 8 : rows + 16, :] = jnp.zeros((8, LANES), F32)
    turned[8 : rows + 8, :] = jnp.concatenate([fields] * 4, axis=0).T
    group = iota((32, LANES), 1) // 32
    for j in range(3):
        chunk = None
        for q in range(4):
            part = turned[pl.ds(6 + 4 * j + q, 32, stride=8), :]
            chunk = part if q == 0 else jnp.where(group == q, part, chunk)
        msg[pl.ds(j, 32, stride=4), :] = chunk
    place = place_in[...].astype(F32)
    msg[pl.ds(3, 16, stride=8), :] = place
    msg[pl.ds(7, 16, stride=8), :] = pltpu.roll(place, 64, 1)
    for c in codes:
        c.wait()
    near[4 * HALO :, :] = code_edge[0].astype(F32)
    far[4 * HALO :, :] = code_edge[1].astype(F32)
    for c in copies:
        c.wait()


def route_kernel(
    land, head_init, sub_init, conduct, drain, code, near, far, share, slot,
    precip, pet, soil_init, ksat, land_mask,
    head_out, sub_out, msg, soil_out,
    turned, h_a, h_b, s_a, s_b, g_w, a_w, dn_w, up_w, rt_w, lf_w, kp_w,
    head, sub, shares, slots, parts, fields_in, mask_in, soil, shifted, sem,
):
    tiles = g_w.shape[0]
    width = tiles * LANES
    zero = jnp.zeros((ROWS, LANES), F32)
    share_copy = pltpu.make_async_copy(share, shares, sem.at[0])
    slot_copy = pltpu.make_async_copy(slot, slots, sem.at[3])
    local = [pltpu.make_async_copy(land_mask, mask_in, sem.at[8])]
    for i, ref in enumerate((precip, pet, soil_init, ksat)):
        local.append(pltpu.make_async_copy(ref, fields_in.at[i], sem.at[4 + i]))
    share_copy.start()
    slot_copy.start()
    for c in local:
        c.start()

    odd = (lax.axis_index("tile") & 1) == 1

    def above(field, at):
        rows = slice(HALO * field, HALO * field + HALO)
        return jnp.where(odd, near[rows, at], far[rows, at])

    def below(field, at):
        rows = slice(HALO * field, HALO * field + HALO)
        return jnp.where(odd, far[rows, at], near[rows, at])

    def window(own, field, j):
        at = cut(j)
        return jnp.concatenate(
            [above(field, at), own[:, at].astype(F32), below(field, at)], axis=0
        )

    for j in range(tiles):
        g_w[j] = window(conduct, 2, j)
        d = window(drain, 3, j)
        k = window(code, 4, j)
        moves = [jnp.where(k == float(i), d, 0.0) for i in range(4)]
        dn_w[j] = pltpu.roll(moves[0], 1, 0)
        up_w[j] = pltpu.roll(moves[1], ROWS - 1, 0)
        rt_w[j] = moves[2]
        lf_w[j] = moves[3]
        kp_w[j] = 1.0 - (moves[0] + moves[1] + moves[2] + moves[3])
    for j in range(tiles):
        g = g_w[j]
        left = pltpu.roll(g_w[j - 1], 1, 1) if j > 0 else zero
        right = pltpu.roll(g_w[j + 1], LANES - 1, 1) if j < tiles - 1 else zero
        total = pltpu.roll(g, 1, 0) + pltpu.roll(g, ROWS - 1, 0)
        total = total + left_of(pltpu.roll(g, 1, 1), left)
        total = total + right_of(pltpu.roll(g, LANES - 1, 1), right)
        a_w[j] = 1.0 - g * total

    data = jnp.concatenate([land[pl.ds(j, 32, stride=4), :] for j in range(3)], axis=1)
    a, b, c = split3(data)
    turned[...] = jnp.concatenate([a, b, c, jnp.zeros_like(a)], axis=0).T
    lhs = jnp.concatenate([turned[pl.ds(q, 24, stride=16), :] for q in range(16)], axis=0)
    lhs = lhs.astype(BF16)
    low_half = iota((8, 256), 0) < 4
    src = iota((LANES, 256), 0)
    dst = iota((LANES, 256), 1)
    col = (iota((24, 256), 1) & 63) >> 2
    for n in range(width // 256):
        hot = ((src & 31) == ((dst + 256 * n) >> 6)) & (src < 96)
        spread = jnp.dot(lhs, jnp.where(hot, 1.0, 0.0).astype(BF16), preferred_element_type=F32)
        fine = spread[0:24]
        for q in range(1, 16):
            fine = jnp.where(col == q, spread[24 * q : 24 * q + 24], fine)
        for i in range(ROWS // 8):
            here = slice(8 * i, 8 * i + 8)
            at = slice(256 * n, 256 * n + 256)
            if i == 0:
                h0, s0 = above(0, at), above(1, at)
            elif i == ROWS // 8 - 1:
                h0, s0 = below(0, at), below(1, at)
            else:
                rows = slice(8 * i - 8, 8 * i)
                h0, s0 = head_init[rows, at], sub_init[rows, at]
            r = 4 * i
            h0 = h0 + jnp.where(low_half, fine[r : r + 1], fine[r + 2 : r + 3])
            s0 = s0 + jnp.where(low_half, fine[r + 1 : r + 2], fine[r + 3 : r + 4])
            for u in range(2):
                j = 2 * n + u
                h_a[j, here, :] = h0[:, cut(u)]
                s_a[j, 8 * i + 8 : 8 * i + 16, :] = s0[:, cut(u)]

    edge = jnp.zeros((tiles, 8, LANES), F32)
    for ref in (shifted, s_a, s_b):
        ref[:, 0:8, :] = edge
        ref[:, ROWS + 8 : ROWS + 16, :] = edge
    middle = slice(8, ROWS + 8)

    def around(keep):
        up_rows = slice(keep.start + 7, keep.stop + 7)
        down_rows = slice(keep.start + 9, keep.stop + 9)
        return up_rows, down_rows

    def head_step(h_in, keep, take):
        above_at, below_at = around(keep)

        def products(j):
            p = g_w[j] * h_in[j]
            return p, pltpu.roll(p, 1, 1), pltpu.roll(p, LANES - 1, 1)

        before = zero
        now = products(0)
        for j in range(tiles):
            after = products(j + 1) if j < tiles - 1 else (zero,) * 3
            shifted[j, middle, :] = now[0]
            flux = shifted[j, above_at, :] + shifted[j, below_at, :]
            flux = flux + left_of(now[1], before)[keep]
            flux = flux + right_of(now[2], after[2])[keep]
            take(j, a_w[j, keep, :] * h_in[j, keep, :] + g_w[j, keep, :] * flux)
            before, now = now[1], after

    def sub_step(s_in, keep, take):
        above_at, below_at = around(keep)

        def products(j):
            s = s_in[j, middle, :]
            return pltpu.roll(rt_w[j] * s, 1, 1), pltpu.roll(lf_w[j] * s, LANES - 1, 1)

        before = zero
        now = products(0)
        for j in range(tiles):
            after = products(j + 1) if j < tiles - 1 else (zero,) * 2
            s = s_in[j, middle, :]
            new = dn_w[j, keep, :] * s_in[j, above_at, :] + up_w[j, keep, :] * s_in[j, below_at, :]
            new = new + left_of(now[0], before)[keep]
            new = new + right_of(now[1], after[1])[keep]
            take(j, new + kp_w[j, keep, :] * s[keep])
            before, now = now[0], after

    def store(to, rows):
        def take(j, x):
            to[j, rows, :] = x

        return take

    def finish_sub(j, s):
        sub[:, cut(j)] = s

    def finish(j, h):
        at = cut(j)
        inflow = shares[:, at] * h
        head[:, at] = h - inflow
        coarse = inflow.astype(BF16).astype(F32)
        parts[0, :, at] = coarse
        parts[1, :, at] = inflow - coarse

    source = (h_a, s_a)
    target = (h_b, s_b)
    for i in range(ITERS - 1):
        sub_step(source[1], slice(0, ROWS), store(target[1], middle))
        source, target = target, source
    sub_step(source[1], slice(HALO, HALO + OWN), finish_sub)
    sub_copy = pltpu.make_async_copy(sub, sub_out, sem.at[2])
    sub_copy.start()
    for c in local:
        c.wait()
    mask = mask_in[...].astype(F32)
    p, s0 = fields_in[0], fields_in[2]
    runoff, drainage = water(p, s0, fields_in[3], mask)
    evap = mask * fields_in[1] * (2.0 * s0)
    soil[...] = s0 + 0.1 * (mask * p - runoff - drainage - evap)
    soil_copy = pltpu.make_async_copy(soil, soil_out, sem.at[9])
    soil_copy.start()
    share_copy.wait()
    slot_copy.wait()
    parts[2] = (slots[...] >> 6).astype(F32)
    parts[3] = (slots[...] & 63).astype(F32)
    source, target = (h_a, s_a), (h_b, s_b)
    for i in range(ITERS - 1):
        head_step(source[0], slice(0, ROWS), store(target[0], slice(0, ROWS)))
        source, target = target, source
    head_step(source[0], slice(HALO, HALO + OWN), finish)
    head_copy = pltpu.make_async_copy(head, head_out, sem.at[1])
    head_copy.start()

    owner = iota((32, width), 0).astype(F32).astype(BF16)
    place = iota((64, width), 0).astype(F32).astype(BF16)
    one = jnp.ones((64, width), BF16)
    none = jnp.zeros((64, width), BF16)

    def wide(i, r, n):
        return jnp.broadcast_to(parts[i, r : r + 1, :], (n, width)).astype(BF16)

    total = jnp.zeros((64, 64), F32)
    for r in range(OWN):
        hi = wide(2, r, 32) == owner
        lhs = jnp.concatenate([jnp.where(hi, wide(i, r, 32), none[0:32]) for i in range(2)], axis=0)
        rhs = jnp.where(wide(3, r, 64) == place, one, none)
        total = total + lax.dot_general(
            lhs, rhs, (((1,), (1,)), ((), ())), preferred_element_type=F32
        )
    total = total[0:32] + total[32:64]
    msg[...] = jnp.concatenate([total, jnp.zeros_like(total)], axis=1)
    soil_copy.wait()
    head_copy.wait()
    sub_copy.wait()


def reach_kernel(land, got, out):
    low = iota((16, LANES), 1) < 64

    def pack(x):
        return jnp.where(low, x[0:16], pltpu.roll(x[16:32], 64, 1))

    sums = pack(got[...])
    place = pack(land[pl.ds(3, 32, stride=4), :]).astype(jnp.int32)

    def line(x):
        return jnp.concatenate([x[u : u + 1] for u in range(16)], axis=1)

    width = 16 * LANES
    hi = line((place >> 7).astype(F32)) == iota((16, width), 0).astype(F32)
    lhs = jnp.concatenate([jnp.where(hi, line(x), 0.0) for x in split3(sums)], axis=0)
    lo = line((place & 127).astype(F32)) == iota((LANES, width), 0).astype(F32)
    total = lax.dot_general(
        lhs.astype(BF16), jnp.where(lo, 1.0, 0.0).astype(BF16),
        (((1,), (1,)), ((), ())), preferred_element_type=F32,
    )
    out[...] = total[0:16] + total[16:32] + total[32:48]


def local(
    precip,
    pet,
    soil_init,
    ksat,
    land_mask,
    head_init,
    subsurface_init,
    conduct,
    drain_rate,
    flow_code,
    channel_share,
    cell_slot,
    slot_reach,
):
    vmem = pl.BlockSpec(memory_space=pltpu.VMEM)
    outside = pl.BlockSpec(memory_space=pltpu.HBM)
    peers = lax.axis_size("tile")
    width = head_init.shape[1]
    tiles = width // LANES

    def hbm(x):
        return pltpu.with_memory_space_constraint(x, pltpu.HBM)

    def array(*shape):
        return jax.ShapeDtypeStruct(shape, F32)

    msg, near, far = pl.pallas_call(
        send_kernel,
        out_shape=(
            array(4 * peers, LANES), array(40, width), array(40, width),
        ),
        in_specs=[outside] * 10,
        out_specs=(vmem,) * 3,
        scratch_shapes=[
            pltpu.VMEM((precip.shape[1] + 16, LANES), F32),
            pltpu.VMEM((3,) + precip.shape, F32),
            pltpu.VMEM(precip.shape, jnp.int32),
            pltpu.VMEM((16, LANES), jnp.int32),
            pltpu.VMEM((2, 8, width), jnp.int32),
            pltpu.SemaphoreType.DMA((16,)),
        ],
        compiler_params=pltpu.CompilerParams(vmem_limit_bytes=6 * MIB),
        name="send",
    )(
        *map(
            hbm,
            (
                precip, soil_init, ksat, land_mask, slot_reach.reshape(-1, LANES),
                head_init, subsurface_init, conduct, drain_rate, flow_code,
            ),
        )
    )
    near = lax.ppermute(near, "tile", [(i, i ^ 1) for i in range(peers)])
    far = lax.ppermute(far, "tile", [(i, ((i + 1) ^ 1) - 1) for i in range(1, peers - 1)])
    land = lax.all_to_all(
        msg.reshape(peers, 4, LANES), "tile", split_axis=0, concat_axis=0, tiled=True
    ).reshape(4 * peers, LANES)

    window = pltpu.VMEM((tiles, ROWS, LANES), F32)
    plane = pltpu.VMEM((OWN, width), F32)
    head, sub, sums, soil = pl.pallas_call(
        route_kernel,
        out_shape=(
            array(OWN, width), array(OWN, width), array(peers, LANES), array(*precip.shape),
        ),
        in_specs=[vmem] * 8 + [outside] * 7,
        out_specs=(outside, outside, vmem, outside),
        scratch_shapes=[pltpu.VMEM((384, LANES), F32)]
        + [window] * 2
        + [pltpu.VMEM((tiles, ROWS + 16, LANES), F32)] * 2
        + [window] * 7
        + [plane] * 3
        + [pltpu.VMEM((OWN, width), jnp.int32), pltpu.VMEM((4, OWN, width), F32)]
        + [pltpu.VMEM((4,) + precip.shape, F32), pltpu.VMEM(precip.shape, jnp.int32)]
        + [pltpu.VMEM(precip.shape, F32), pltpu.VMEM((tiles, ROWS + 16, LANES), F32)]
        + [pltpu.SemaphoreType.DMA((10,))],
        compiler_params=pltpu.CompilerParams(vmem_limit_bytes=16 * MIB),
        name="route",
    )(
        land, head_init, subsurface_init, conduct, drain_rate, flow_code, near, far,
        *map(hbm, (channel_share, cell_slot, precip, pet, soil_init, ksat, land_mask)),
    )
    sums = lax.all_to_all(sums, "tile", split_axis=0, concat_axis=0, tiled=True)
    reach = pl.pallas_call(
        reach_kernel,
        out_shape=array(16, LANES),
        in_specs=[vmem] * 2,
        out_specs=vmem,
        compiler_params=pltpu.CompilerParams(vmem_limit_bytes=6 * MIB),
        name="reach_sums",
    )(land, sums)
    return (soil, head, sub, reach.reshape(-1))


def solution(mesh):
    rows = P(("member", "tile"), None)
    flat = P(("member", "tile"))
    return jax.shard_map(
        local,
        mesh=mesh,
        in_specs=(rows,) * 12 + (flat,),
        out_specs=(rows, rows, rows, flat),
        check_vma=False,
    )
```
